256 devices in a mesh: sector: 64 (over z, x, y_hi), band: 4 (over y_lo, core).
Axes of the slice: x: 4, y: 4 (y_hi: 2, y_lo: 2; y = y_hi * 2 + y_lo), z: 8, core: 2. Of those that a mesh axis runs over, the one named last changes fastest.
Arguments:
- given_load: float32 [3, 512, 64, 256], P(None, 'sector', 'band'), may hold values from -20 to 20, as said below
- displacement: float32 [3, 512, 64, 256], P(None, 'sector', 'band'), may hold values from -3 to 3
- mass_coef: float32 [512, 64, 256], P('sector', 'band'), may hold values from 0.05 to 0.5
- stiffness: float32 [512, 64, 256], P('sector', 'band'), may hold values from 0.5 to 2
- bearing_node: int32 [1024], P(('sector', 'band')), may hold values from 0 to 2047
- stick_state: int32 [1024], P(('sector', 'band')), may hold values 0 or 1
- slip_prev: float32 [2, 1024], P(None, ('sector', 'band')), may hold values from -3 to 3
- bearing_old: float32 [2, 1024], P(None, ('sector', 'band')), may hold values from -3 to 3
- bearing_weight: float32 [1024], P(('sector', 'band')), may hold values from 4 to 16
Outputs:
- increment: float32 [3, 512, 64, 256], P(None, 'sector', 'band')
- cg_residual: float32 [3, 512, 64, 256], P(None, 'sector', 'band')
- bearing_force: float32 [3, 1024], P(None, ('sector', 'band'))
The draws below stay inside these ranges and needn't reach their ends.
Inputs may be any that keep to these rules, and one draw needn't show every extreme that they name: `bearing_node`: each index names a node of the raft-base layer within the bearing's own sector; several bearings may share a node. `given_load`: loads of order one to a few tens.
All inputs are finite; a program needn't handle non-finite values. No bound on the sum of `stick_state` on one device may be relied on, other than what follows from the above.
Results may differ from the reference program's by a relative error of at most 0.00021.
Values sent between devices are 32-bit elements; how exact they have to be, the bound alone decides.
A program may use at most 64 MiB of HBM per device.

```python
import math
import jax
import jax.numpy as jnp

CA = 8
NR = 256
ITERS = 4
BEAR_DEV = 4
NA = 512
NH = 64
NB = 1024
N_SECTOR = 64
N_BAND = 4


def draw_given_load(key, part):
    key_base = jax.random.fold_in(key, 0)
    ramp = 1.0 + 2.0 * jnp.arange(NA, dtype=jnp.float32) / max(NA - 1, 1)
    ramp = ramp[None, :, None, None]
    base = jax.random.normal(key_base, (3, NA, NH, NR), jnp.float32)
    values = ramp * jnp.clip(base, -6.0, 6.0)
    return values.astype(jnp.float32)


def place_ends(values, rng, smallest, largest):
    longest = values.shape.index(max(values.shape))
    spots = []
    for shift in (0, 1):
        where = [jax.random.randint(jax.random.fold_in(rng, axis), (), 0, length) for axis, length in enumerate(values.shape)]
        where[longest] = (where[longest] + shift) % values.shape[longest]
        spots.append(tuple(where))
    return values.at[spots[0]].set(smallest).at[spots[1]].set(largest)


def steps_of(rng, dims, cuts, smallest, largest):
    gain = 1.0
    for axis_at, shards_of in cuts:
        draws = jax.random.uniform(jax.random.fold_in(jax.random.fold_in(rng, 6), axis_at), (shards_of,), jnp.float32, smallest / len(cuts), largest / len(cuts))
        gain = gain * jnp.repeat(jnp.exp(draws), dims[axis_at] // shards_of).reshape((-1,) + (1,) * (len(dims) - 1 - axis_at))
    return gain


def centred(own_key, shape, scale, bound, cuts=(), kind=jnp.bfloat16):
    values = scale * jax.random.normal(own_key, shape, jnp.float32)
    if cuts:
        values = values * steps_of(own_key, shape, cuts, -0.22, 0.18)
    return jnp.clip(values, -bound, bound).astype(kind)


def setup_inputs(seed: int = 0) -> dict:
    key_list = jax.random.split(jax.random.key(seed), 10)
    given_load = draw_given_load(jax.random.fold_in(key_list[9], 71), 0)
    displacement = centred(key_list[1], (3, NA, NH, NR), 0.5, 3.0, ((1, 64), (2, 4)), jnp.float32)
    mass_coef = jnp.clip(jnp.exp(math.log(0.5) - 2.3025851 * jax.random.uniform(key_list[2], (NA, NH, NR), jnp.float32) ** steps_of(key_list[2], (NA, NH, NR), ((0, 64), (1, 4)), -0.2, 0.2)), 0.05, 0.5)
    stiffness = jnp.clip(jnp.exp(math.log(2.0) - 1.3862944 * jax.random.uniform(key_list[3], (NA, NH, NR), jnp.float32) ** steps_of(key_list[3], (NA, NH, NR), ((0, 64), (1, 4)), -0.2, 0.2)), 0.5, 2.0)
    bearing_node = place_ends(jax.random.randint(key_list[4], (NB,), 0, CA * NR), jax.random.fold_in(key_list[4], 1), 0, (CA * NR) - 1).astype(jnp.int32)
    stick_state = place_ends((jax.random.randint(key_list[5], (NB,), 0, 2) < 1).astype(jnp.int32), jax.random.fold_in(key_list[5], 1), 0, 1)
    slip_prev = centred(key_list[6], (2, NB), 0.5, 3.0, ((1, 256),), jnp.float32)
    bearing_old = centred(key_list[7], (2, NB), 0.5, 3.0, ((1, 256),), jnp.float32)
    bearing_weight = jnp.clip(jnp.exp(math.log(16.0) - 1.3862944 * jax.random.uniform(key_list[8], (NB,), jnp.float32) ** steps_of(key_list[8], (NB,), ((0, 256),), -0.2, 0.2)), 4.0, 16.0)
    return dict(given_load=given_load, displacement=displacement, mass_coef=mass_coef, stiffness=stiffness, bearing_node=bearing_node, stick_state=stick_state, slip_prev=slip_prev, bearing_old=bearing_old, bearing_weight=bearing_weight)


K_STICK = 4.0
K_VERT = 8.0
MU_FAST = 0.15
MU_SLOW = 0.04
RATE_GAIN = 2.0
RATE_DECAY = 2.0
V_FLOOR = 0.05
COMPONENT_SCALE = (1.0, 1.0, 2.0)

def face_conductance(left, right):
    return 2.0 * left * right / (left + right)

def conductances(stiffness):
    cycle_padded = jnp.concatenate([stiffness[-1:], stiffness, stiffness[:1]], axis=0)
    cond_sector = face_conductance(cycle_padded[:-1], cycle_padded[1:])
    height_padded = jnp.pad(stiffness, ((0, 0), (1, 1), (0, 0)))
    cond_height = face_conductance(height_padded[:, :-1], height_padded[:, 1:])
    cond_radial = face_conductance(stiffness[:, :, :-1], stiffness[:, :, 1:])
    return (cond_sector, cond_height, cond_radial)

def operate(field, mass_coef, conds, bottom_diag):
    cond_sector, cond_height, cond_radial = conds
    scales = jnp.array(COMPONENT_SCALE, jnp.float32)[:, None, None, None]
    cycle_padded = jnp.concatenate([field[:, -1:], field, field[:, :1]], axis=1)
    flux_sector = cond_sector[None] * (cycle_padded[:, 1:] - cycle_padded[:, :-1])
    total = -(flux_sector[:, 1:] - flux_sector[:, :-1])
    height_padded = jnp.pad(field, ((0, 0), (0, 0), (1, 1), (0, 0)))
    flux_height = cond_height[None] * (height_padded[:, :, 1:] - height_padded[:, :, :-1])
    total = total - (flux_height[:, :, 1:] - flux_height[:, :, :-1])
    flux_radial = cond_radial[None] * (field[..., 1:] - field[..., :-1])
    flux_radial = jnp.pad(flux_radial, ((0, 0), (0, 0), (0, 0), (1, 1)))
    total = total - (flux_radial[..., 1:] - flux_radial[..., :-1])
    layers = field.shape[2]
    diag_full = jnp.pad(bottom_diag[:, :, None, :], ((0, 0), (0, 0), (0, layers - 1), (0, 0)))
    return mass_coef[None] * field + scales * total + diag_full * field

def bearing_law(at_node, stick_state, slip_prev, bearing_old, bearing_weight):
    moved = at_node[:2]
    trial = K_STICK * (moved - slip_prev)
    slip_rate = RATE_GAIN * (moved - bearing_old)
    slip_speed = jnp.sqrt(slip_rate[0] * slip_rate[0] + slip_rate[1] * slip_rate[1] + V_FLOOR * V_FLOOR)
    friction = MU_FAST - (MU_FAST - MU_SLOW) * jnp.exp(-RATE_DECAY * slip_speed)
    capacity = friction * bearing_weight
    magnitude = jnp.sqrt(trial[0] * trial[0] + trial[1] * trial[1])
    sliding = capacity[None] * trial / jnp.maximum(magnitude, capacity)[None]
    sticking = stick_state[None] == 1
    horizontal = jnp.where(sticking, trial, sliding)
    vertical = K_VERT * at_node[2]
    force = jnp.concatenate([horizontal, vertical[None]], axis=0)
    stick_k = jnp.where(stick_state == 1, K_STICK, 0.0).astype(jnp.float32)
    stiff = jnp.stack([stick_k, stick_k, jnp.full_like(stick_k, K_VERT)], axis=0)
    return (force, stiff)

def reference(given_load, displacement, mass_coef, stiffness, bearing_node, stick_state, slip_prev, bearing_old, bearing_weight):
    conds = conductances(stiffness)
    raft = displacement[:, :, 0, :].reshape(3, N_SECTOR, CA * NR)
    sector_of = (jnp.arange(NB, dtype=jnp.int32) // (BEAR_DEV * N_BAND)).astype(jnp.int32)
    at_node = raft[:, sector_of, bearing_node]
    force, stiff = bearing_law(at_node, stick_state, slip_prev, bearing_old, bearing_weight)
    loads = jnp.zeros((3, N_SECTOR, CA * NR), jnp.float32).at[:, sector_of, bearing_node].add(force)
    bottom = jnp.zeros((3, N_SECTOR, CA * NR), jnp.float32).at[:, sector_of, bearing_node].add(stiff)
    loads = loads.reshape(3, NA, NR)
    bottom = bottom.reshape(3, NA, NR)
    zero_diag = jnp.zeros((3, NA, NR), jnp.float32)
    load_full = jnp.pad(loads[:, :, None, :], ((0, 0), (0, 0), (0, NH - 1), (0, 0)))
    newton_rhs = given_load - operate(displacement, mass_coef, conds, zero_diag) - load_full
    increment = jnp.zeros_like(newton_rhs)
    residual = newton_rhs
    direction = newton_rhs
    norm_now = jnp.sum(residual * residual)
    for iteration in range(ITERS):
        image = operate(direction, mass_coef, conds, bottom)
        alpha = norm_now / jnp.sum(direction * image)
        increment = increment + alpha * direction
        residual = residual - alpha * image
        norm_next = jnp.sum(residual * residual)
        direction = residual + norm_next / norm_now * direction
        norm_now = norm_next
    return (increment, residual, force)
```

```python
import functools

import jax
import jax.numpy as jnp
from jax import lax
from jax.experimental import pallas as pl
from jax.experimental.pallas import tpu as pltpu
from jax.sharding import PartitionSpec as P

ITERS = 4
K_STICK = 4.0
K_VERT = 8.0
MU_FAST = 0.15
MU_SLOW = 0.04
RATE_GAIN = 2.0
RATE_DECAY = 2.0
V_FLOOR = 0.05
HIGHEST = lax.Precision.HIGHEST
MESH = pl.DeviceIdType.MESH

C = 14.0
E = 14.0
CA = 8
LAYERS = 16
NR = 256
DEPTH = 4
ROWS = CA + 2 * DEPTH
LEV = LAYERS + 2 * DEPTH
N_SECTOR = 64
N_BAND = 4
NX = 4
NZ = 8
PAIRS = [(0, 0), (0, 1), (1, 1), (0, 2), (1, 2), (2, 2), (0, 3), (1, 3), (2, 3), (3, 3), (0, 4), (1, 4), (2, 4), (3, 4)]


def coefficients(gram):
    def apply(d):
        q = [None] * 5

        def add(k, v):
            q[k] = v if q[k] is None else q[k] + v

        for j, dj in enumerate(d):
            add(j, C * dj)
            if j == 0:
                add(1, E * dj)
            else:
                add(j + 1, (E / 2) * dj)
                add(j - 1, (E / 2) * dj)
        return [v for v in q if v is not None]

    def inner(a, b):
        total = None
        for i, ai in enumerate(a):
            for j, bj in enumerate(b):
                term = ai * bj * gram(min(i, j), max(i, j))
                total = term if total is None else total + term
        return total

    def padded_add(a, b, scale):
        out = []
        for i in range(max(len(a), len(b))):
            if i >= len(a):
                out.append(scale * b[i])
            elif i >= len(b):
                out.append(a[i])
            else:
                out.append(a[i] + scale * b[i])
        return out

    one = jnp.ones_like(gram(0, 0))
    r, d, x = [one], [one], []
    rr = gram(0, 0)
    for k in range(ITERS):
        q = apply(d)
        alpha = rr / inner(d, q)
        x = padded_add(x, d, alpha)
        r = padded_add(r, q, -alpha)
        if k < ITERS - 1:
            new = inner(r, r)
            d = padded_add(r, d, new / rr)
            rr = new
    return x, r


def kernel(
    load_hbm,
    disp_hbm,
    mass_hbm,
    stiff_hbm,
    node_ref,
    stick_ref,
    slip_ref,
    old_ref,
    weight_ref,
    inc_ref,
    res_ref,
    force_ref,
    st,
    me,
    u,
    p,
    k_row,
    k_up,
    k_dn,
    k_in,
    k_out,
    diag,
    bdiag,
    loads,
    pack,
    packs,
    forces,
    force_in,
    gtile,
    red_a,
    red_b,
    red_c,
    load_sem,
    send_sem,
    recv_sem,
    pack_send,
    pack_recv,
    force_send,
    force_recv,
    ra_send,
    ra_recv,
    rb_send,
    rb_recv,
    rc_send,
    rc_recv,
):
    s = lax.axis_index("sector")
    b = lax.axis_index("band")
    z, x, yh = s // 8, lax.rem(s // 2, 4), lax.rem(s, 2)
    s_dn, s_up = lax.rem(s + N_SECTOR - 1, N_SECTOR), lax.rem(s + 1, N_SECTOR)
    low, high = b == 0, b == N_BAND - 1

    group_a = []
    for da in range(2):
        for db in range(4):
            if (da, db) != (0, 0):
                group_a.append(((s // 2) * 2 + lax.rem(yh + da, 2), lax.rem(b + db, 4)))
    group_b = [((z * 4 + lax.rem(x + i, 4)) * 2 + yh, b) for i in range(1, NX)]
    group_c = [((lax.rem(z + i, 8) * 4 + x) * 2 + yh, b) for i in range(1, NZ)]

    local = [
        pltpu.make_async_copy(stiff_hbm, st.at[0:CA, 0:LAYERS, :], load_sem.at[0]),
        pltpu.make_async_copy(disp_hbm, u.at[:, 0:CA, 0:LAYERS, :], load_sem.at[1]),
        pltpu.make_async_copy(mass_hbm, me.at[0:CA, 0:LAYERS, :], load_sem.at[2]),
        pltpu.make_async_copy(load_hbm, p.at[0, :, 0:CA, 0:LAYERS, :], load_sem.at[3]),
    ]
    for copy in local:
        copy.start()

    barrier = pltpu.get_barrier_semaphore()
    everyone = [(s_dn, b), (s_up, b)] + group_a + group_b + group_c
    for target in everyone:
        pl.semaphore_signal(barrier, inc=1, device_id=target, device_id_type=MESH)

    pack[...] = jnp.zeros_like(pack)
    pack[0:1, 0:4] = node_ref[...].astype(jnp.float32)
    pack[1:2, 0:4] = stick_ref[...].astype(jnp.float32)
    pack[2:4, 0:4] = slip_ref[...]
    pack[4:6, 0:4] = old_ref[...]
    pack[6:7, 0:4] = weight_ref[...]

    @pl.when(low)
    def _():
        st[:, LEV - DEPTH : LEV, :] = jnp.zeros((ROWS, DEPTH, NR), jnp.float32)
        me[:, LEV - DEPTH : LEV, :] = jnp.zeros((ROWS, DEPTH, NR), jnp.float32)
        u[:, 0:CA, LEV - 1 : LEV, :] = jnp.zeros((3, CA, 1, NR), jnp.float32)
        p[0, :, :, LEV - DEPTH : LEV, :] = jnp.zeros((3, ROWS, DEPTH, NR), jnp.float32)

    @pl.when(high)
    def _():
        st[:, LAYERS : LAYERS + DEPTH, :] = jnp.zeros((ROWS, DEPTH, NR), jnp.float32)
        me[:, LAYERS : LAYERS + DEPTH, :] = jnp.zeros((ROWS, DEPTH, NR), jnp.float32)
        u[:, 0:CA, LAYERS : LAYERS + 1, :] = jnp.zeros((3, CA, 1, NR), jnp.float32)
        p[0, :, :, LAYERS : LAYERS + DEPTH, :] = jnp.zeros((3, ROWS, DEPTH, NR), jnp.float32)

    def remote(i, src, dst, target):
        return pltpu.make_async_remote_copy(
            src_ref=src,
            dst_ref=dst,
            send_sem=send_sem.at[i],
            recv_sem=recv_sem.at[i],
            device_id=target,
            device_id_type=MESH,
        )

    own, rim = slice(0, CA), slice(CA, ROWS)
    first, last = slice(0, DEPTH), slice(CA - DEPTH, CA)
    after, before = slice(CA, CA + DEPTH), slice(CA + DEPTH, ROWS)
    lay = slice(0, LAYERS)
    bottom, top = slice(0, DEPTH), slice(LAYERS - DEPTH, LAYERS)
    above, below = slice(LAYERS, LAYERS + DEPTH), slice(LAYERS + DEPTH, LEV)

    b_dn, b_up = (s, lax.rem(b + N_BAND - 1, N_BAND)), (s, lax.rem(b + 1, N_BAND))
    t_dn, t_up = (s_dn, b), (s_up, b)

    u_down = remote(8, disp_hbm.at[:, :, 0:1, :], u.at[:, own, LAYERS : LAYERS + 1, :], b_dn)
    u_up = remote(9, disp_hbm.at[:, :, LAYERS - 1 : LAYERS, :], u.at[:, own, LEV - 1 : LEV, :], b_up)
    st_down = remote(6, stiff_hbm.at[:, bottom, :], st.at[own, above, :], b_dn)
    st_up = remote(7, stiff_hbm.at[:, top, :], st.at[own, below, :], b_up)
    me_down = remote(10, mass_hbm.at[:, bottom, :], me.at[own, above, :], b_dn)
    me_up = remote(11, mass_hbm.at[:, top, :], me.at[own, below, :], b_up)
    st_first = remote(0, stiff_hbm.at[first], st.at[after, lay, :], t_dn)
    st_last = remote(1, stiff_hbm.at[last], st.at[before, lay, :], t_up)
    me_first = remote(2, mass_hbm.at[first], me.at[after, lay, :], t_dn)
    me_last = remote(3, mass_hbm.at[last], me.at[before, lay, :], t_up)
    u_first = remote(4, disp_hbm.at[:, 0:1], u.at[:, CA : CA + 1, lay, :], t_dn)
    u_last = remote(5, disp_hbm.at[:, CA - 1 : CA], u.at[:, ROWS - 1 : ROWS, lay, :], t_up)
    st_rim_down = remote(12, st.at[rim, bottom, :], st.at[rim, above, :], b_dn)
    st_rim_up = remote(13, st.at[rim, top, :], st.at[rim, below, :], b_up)
    me_rim_down = remote(14, me.at[rim, bottom, :], me.at[rim, above, :], b_dn)
    me_rim_up = remote(15, me.at[rim, top, :], me.at[rim, below, :], b_up)
    bd_first = remote(16, bdiag.at[:, first, :], bdiag.at[:, after, :], t_dn)
    bd_last = remote(17, bdiag.at[:, last, :], bdiag.at[:, before, :], t_up)
    p_first = remote(18, p.at[0, :, first, lay, :], p.at[0, :, after, lay, :], t_dn)
    p_last = remote(19, p.at[0, :, last, lay, :], p.at[0, :, before, lay, :], t_up)
    p_down = remote(20, p.at[0, :, :, bottom, :], p.at[0, :, :, above, :], b_dn)
    p_up = remote(21, p.at[0, :, :, top, :], p.at[0, :, :, below, :], b_up)

    def pack_copy(slot):
        return pltpu.make_async_remote_copy(
            src_ref=pack,
            dst_ref=packs.at[slot],
            send_sem=pack_send.at[slot],
            recv_sem=pack_recv.at[slot],
            device_id=(s, 0),
            device_id_type=MESH,
        )

    def force_copy(slot):
        return pltpu.make_async_remote_copy(
            src_ref=forces.at[slot],
            dst_ref=force_in,
            send_sem=force_send.at[slot],
            recv_sem=force_recv.at[0],
            device_id=(s, slot),
            device_id_type=MESH,
        )

    def downward(*copies):
        @pl.when(jnp.logical_not(low))
        def _():
            for copy in copies:
                copy.start()

    def upward(*copies):
        @pl.when(jnp.logical_not(high))
        def _():
            for copy in copies:
                copy.start()

    def from_bands(downs, ups):
        @pl.when(jnp.logical_not(high))
        def _():
            for copy in downs:
                copy.wait_recv()

        @pl.when(jnp.logical_not(low))
        def _():
            for copy in ups:
                copy.wait_recv()

    pl.semaphore_wait(barrier, len(everyone))

    for slot in range(1, N_BAND):

        @pl.when(b == slot)
        def _():
            pack_copy(slot).start()

    downward(u_down, st_down)
    upward(u_up, st_up)
    for copy in (st_first, st_last, u_first, u_last, me_first, me_last):
        copy.start()
    downward(me_down)
    upward(me_up)

    def face(a, c):
        return (4.0 / E) * a * c / jnp.maximum(a + c, 0.25)

    lane = lax.broadcasted_iota(jnp.int32, (LEV, NR), 1)

    def conductances_of(i):
        a = st[i]
        ku = face(a, pltpu.roll(a, LEV - 1, 0))
        ko = jnp.where(lane == NR - 1, 0.0, face(a, pltpu.roll(a, NR - 1, 1)))
        k_up[i] = ku
        k_dn[i] = pltpu.roll(ku, 1, 0)
        k_out[i] = ko
        k_in[i] = pltpu.roll(ko, 1, 1)

    local[0].wait()
    from_bands([u_down, st_down], [u_up, st_up])

    @pl.loop(0, CA)
    def _(i):
        conductances_of(i)

    @pl.loop(0, CA - 1)
    def _(i):
        k_row[i] = face(st[i], st[i + 1])

    local[1].wait()
    local[2].wait()
    local[3].wait()

    @pl.when(low)
    def _():
        packs[0] = pack[...]
        for slot in range(1, N_BAND):
            pack_copy(slot).wait_recv()
        t = packs[0]
        for slot in range(1, N_BAND):
            t = t + pltpu.roll(packs[slot], 4 * slot, 1)
        t = t[:, 0:128]
        node = t[0:1, :].astype(jnp.int32)
        stick = t[1:2, :] > 0.5
        row_of = node // NR
        col_of = lax.rem(node, NR)
        real = lax.broadcasted_iota(jnp.int32, (1, 128), 1) < 4 * N_BAND
        col_hot = jnp.where(
            jnp.logical_and(lax.broadcasted_iota(jnp.int32, (NR, 128), 0) == col_of, real), 1.0, 0.0
        ).astype(jnp.float32)
        row_hot = jnp.where(lax.broadcasted_iota(jnp.int32, (CA, 128), 0) == row_of, 1.0, 0.0).astype(jnp.float32)
        raft = jnp.concatenate([u[c, r, 0:1, :] for c in range(3) for r in range(CA)], axis=0)
        picked = jnp.dot(raft, col_hot, precision=HIGHEST, preferred_element_type=jnp.float32)
        at = [jnp.sum(picked[CA * c : CA * (c + 1)] * row_hot, axis=0, keepdims=True) for c in range(3)]
        trial = [K_STICK * (at[c] - t[2 + c : 3 + c]) for c in range(2)]
        rate = [RATE_GAIN * (at[c] - t[4 + c : 5 + c]) for c in range(2)]
        speed = jnp.sqrt(rate[0] * rate[0] + rate[1] * rate[1] + V_FLOOR * V_FLOOR)
        friction = MU_FAST - (MU_FAST - MU_SLOW) * jnp.exp(-RATE_DECAY * speed)
        capacity = friction * t[6:7]
        magnitude = jnp.sqrt(trial[0] * trial[0] + trial[1] * trial[1])
        largest = jnp.maximum(magnitude, capacity)
        largest = jnp.where(real, largest, 1.0)
        force = [jnp.where(stick, trial[c], capacity * trial[c] / largest) for c in range(2)]
        force = [jnp.where(real, f, 0.0) for f in force + [K_VERT * at[2]]]
        stick_k = jnp.where(jnp.logical_and(stick, real), K_STICK, 0.0)
        vert_k = jnp.where(real, K_VERT, 0.0)
        weights = jnp.concatenate([row_hot * v for v in force + [stick_k, vert_k]], axis=0)
        spread = lax.dot_general(
            weights, col_hot, (((1,), (1,)), ((), ())), precision=HIGHEST, preferred_element_type=jnp.float32
        )
        for c in range(3):
            loads[c] = spread[CA * c : CA * (c + 1)]
        bdiag[0, 0:CA] = spread[3 * CA : 4 * CA]
        bdiag[1, 0:CA] = spread[4 * CA : 5 * CA]
        tile = jnp.concatenate(force + [jnp.zeros((5, 128), jnp.float32)], axis=0)
        force_in[...] = tile
        for slot in range(1, N_BAND):
            forces[slot] = pltpu.roll(tile, 128 - 4 * slot, 1)
        for slot in range(1, N_BAND):
            force_copy(slot).start()

    @pl.when(jnp.logical_not(low))
    def _():
        loads[...] = jnp.zeros_like(loads)
        bdiag[:, 0:CA, :] = jnp.zeros((2, CA, NR), jnp.float32)

    bd_first.start()
    bd_last.start()

    gains = (1.0, 1.0, 2.0)
    layer = lax.broadcasted_iota(jnp.int32, (LAYERS, NR), 0)

    @pl.loop(0, CA)
    def _(i):
        up, dn = jnp.minimum(i + 1, CA - 1), jnp.maximum(i - 1, 0)
        on_up = jnp.where(i < CA - 1, 1.0, 0.0)
        kr_up = k_row[jnp.minimum(i, CA - 2), lay, :]
        kr_dn = k_row[dn, lay, :]
        ku, kd, ko, ki = k_up[i, lay, :], k_dn[i, lay, :], k_out[i, lay, :], k_in[i, lay, :]
        m = me[i, lay, :]
        for c in range(3):
            whole = u[c, i]
            v = whole[0:LAYERS]
            above_v = pltpu.roll(whole, LEV - 1, 0)[0:LAYERS]
            below_v = pltpu.roll(whole, 1, 0)[0:LAYERS]
            acc = ku * (above_v - v) + kd * (below_v - v)
            acc = acc + ko * (pltpu.roll(v, NR - 1, 1) - v) + ki * (pltpu.roll(v, 1, 1) - v)
            acc = acc + kr_up * (u[c, up, lay, :] - v) + kr_dn * (u[c, dn, lay, :] - v)
            rhs = p[0, c, i, lay, :] - m * v + (gains[c] * E / 2) * acc
            rhs = rhs - jnp.where(layer == 0, loads[c, pl.ds(i, 1), :], 0.0)
            p[0, c, i, lay, :] = rhs

    p_first.start()
    p_last.start()

    for copy in (st_first, st_last, me_first, me_last):
        copy.wait_recv()
    downward(st_rim_down, me_rim_down)
    upward(st_rim_up, me_rim_up)
    from_bands([me_down, st_rim_down, me_rim_down], [me_up, st_rim_up, me_rim_up])

    @pl.loop(CA, ROWS)
    def _(i):
        conductances_of(i)

    @pl.loop(CA - 1, ROWS)
    def _(i):
        k_row[i] = face(st[i], st[lax.rem(i + 1, ROWS)])

    for copy in (bd_first, bd_last):
        copy.wait_recv()
    lev = lax.broadcasted_iota(jnp.int32, (LEV, NR), 0)

    @pl.loop(0, ROWS)
    def _(i):
        near = k_up[i] + k_dn[i] + k_out[i] + k_in[i] + k_row[i] + k_row[lax.rem(i + ROWS - 1, ROWS)]
        base = (2.0 / E) * (me[i] - C)
        for h in range(2):
            extra = (2.0 / E) * bdiag[h, pl.ds(i, 1), :]
            diag[h, i] = base + (h + 1.0) * near + jnp.where(lev == 0, extra, 0.0)

    for copy in (p_first, p_last):
        copy.wait_send()
    for copy in (u_first, u_last, p_first, p_last):
        copy.wait_recv()
    for here, there, at in ((CA - 1, CA, CA - 1), (0, ROWS - 1, ROWS - 1)):
        for c in range(3):
            flux = (gains[c] * E / 2) * k_row[at, lay, :] * (u[c, there, lay, :] - u[c, here, lay, :])
            p[0, c, here, lay, :] = p[0, c, here, lay, :] + flux
            p[0, c, there, lay, :] = p[0, c, there, lay, :] - flux
    downward(p_down)
    upward(p_up)
    from_bands([p_down], [p_up])

    sums = {}

    def one_row(j, i):
        up, dn = lax.rem(i + 1, ROWS), lax.rem(i + ROWS - 1, ROWS)
        kr_up, kr_dn, ku, kd, ko, ki = k_row[i], k_row[dn], k_up[i], k_dn[i], k_out[i], k_in[i]
        out = []
        for c in range(3):
            v = p[j, c, i]
            near = ku * pltpu.roll(v, LEV - 1, 0) + kd * pltpu.roll(v, 1, 0)
            near = near + ko * pltpu.roll(v, NR - 1, 1) + ki * pltpu.roll(v, 1, 1)
            near = near + kr_up * p[j, c, up] + kr_dn * p[j, c, dn]
            if c == 2:
                near = near + near
            w = diag[c // 2, i] * v - near
            w = 0.5 * w if j == 0 else w - p[j - 1, c, i]
            p[j + 1, c, i] = w
            out.append(w)
        return out

    for j in range(ITERS):
        pairs = [q for q in PAIRS if q[1] == j + 1 or (j == 0 and q == (0, 0))]

        def own_row(i, acc):
            new = one_row(j, i)
            acc = list(acc)
            for c in range(3):
                w = new[c][0:LAYERS]
                for n, (lo, hi) in enumerate(pairs):
                    a = w if lo == j + 1 else p[lo, c, i, lay, :]
                    d = w if hi == j + 1 else p[hi, c, i, lay, :]
                    acc[n] = acc[n] + a * d
            return tuple(acc)

        totals = lax.fori_loop(0, CA, own_row, tuple(jnp.zeros((LAYERS, NR), jnp.float32) for _ in pairs))
        sums.update(zip(pairs, totals))
        wide = ITERS - 1 - j
        if wide:

            @pl.loop(0, 2 * wide)
            def _(i):
                one_row(j, jnp.where(i < wide, CA + i, ROWS - 1 - (i - wide)))

    gtile[...] = jnp.zeros_like(gtile)
    for n, q in enumerate(PAIRS):
        t = jnp.sum(sums[q], axis=0, keepdims=True)
        gtile[n : n + 1, :] = t[:, 0:128] + t[:, 128:256]

    def reduce_over(group, slots, sends, recvs):
        copies = [
            pltpu.make_async_remote_copy(
                src_ref=gtile,
                dst_ref=slots.at[n],
                send_sem=sends.at[n],
                recv_sem=recvs.at[n],
                device_id=target,
                device_id_type=MESH,
            )
            for n, target in enumerate(group)
        ]
        for copy in copies:
            copy.start()
        for copy in copies:
            copy.wait()
        total = gtile[...]
        for n in range(len(group)):
            total = total + slots[n]
        gtile[...] = total

    reduce_over(group_a, red_a, ra_send, ra_recv)
    reduce_over(group_b, red_b, rb_send, rb_recv)
    reduce_over(group_c, red_c, rc_send, rc_recv)
    g = jnp.broadcast_to(jnp.sum(gtile[...], axis=1, keepdims=True), (16, 128))
    where = {q: n for n, q in enumerate(PAIRS)}
    grams = {q: g[where[q] : where[q] + 1, :] for q in PAIRS}
    xs, rs = coefficients(lambda i, j: grams[(i, j)])
    xs = [jnp.concatenate([v, v], axis=1) for v in xs]
    rs = [jnp.concatenate([v, v], axis=1) for v in rs]

    @pl.loop(0, CA)
    def _(i):
        for c in range(3):
            vs = [p[j, c, i, lay, :] for j in range(ITERS + 1)]
            inc, res = xs[0] * vs[0], rs[0] * vs[0]
            for j in range(1, ITERS):
                inc = inc + xs[j] * vs[j]
            for j in range(1, ITERS + 1):
                res = res + rs[j] * vs[j]
            inc_ref[c, i] = inc
            res_ref[c, i] = res

    @pl.when(jnp.logical_not(low))
    def _():
        force_copy(1).wait_recv()

    force_ref[...] = force_in[0:3, 0:4]

    for slot in range(1, N_BAND):

        @pl.when(b == slot)
        def _():
            pack_copy(slot).wait_send()

    @pl.when(low)
    def _():
        for slot in range(1, N_BAND):
            force_copy(slot).wait_send()

    for copy in (st_first, st_last, u_first, u_last, me_first, me_last, bd_first, bd_last):
        copy.wait_send()

    @pl.when(jnp.logical_not(low))
    def _():
        for copy in (u_down, st_down, me_down, st_rim_down, me_rim_down, p_down):
            copy.wait_send()

    @pl.when(jnp.logical_not(high))
    def _():
        for copy in (u_up, st_up, me_up, st_rim_up, me_rim_up, p_up):
            copy.wait_send()


def per_device(
    given_load,
    displacement,
    mass_coef,
    stiffness,
    bearing_node,
    stick_state,
    slip_prev,
    bearing_old,
    bearing_weight,
):
    f32 = jnp.float32
    vmem, dma = pltpu.VMEM, pltpu.SemaphoreType.DMA
    field = jax.ShapeDtypeStruct((3, CA, LAYERS, NR), f32)
    in_vmem = pl.BlockSpec(memory_space=vmem)
    anywhere = pl.BlockSpec(memory_space=pl.ANY)
    return pl.pallas_call(
        kernel,
        out_shape=(field, field, jax.ShapeDtypeStruct((3, 4), f32)),
        in_specs=[anywhere] * 4 + [in_vmem] * 5,
        out_specs=(in_vmem, in_vmem, in_vmem),
        scratch_shapes=[
            vmem((ROWS, LEV, NR), f32),
            vmem((ROWS, LEV, NR), f32),
            vmem((3, ROWS, LEV, NR), f32),
            vmem((ITERS + 1, 3, ROWS, LEV, NR), f32),
            vmem((ROWS, LEV, NR), f32),
            vmem((ROWS, LEV, NR), f32),
            vmem((ROWS, LEV, NR), f32),
            vmem((ROWS, LEV, NR), f32),
            vmem((ROWS, LEV, NR), f32),
            vmem((2, ROWS, LEV, NR), f32),
            vmem((2, ROWS, NR), f32),
            vmem((3, CA, NR), f32),
            vmem((8, 128), f32),
            vmem((N_BAND, 8, 128), f32),
            vmem((N_BAND, 8, 128), f32),
            vmem((8, 128), f32),
            vmem((16, 128), f32),
            vmem((7, 16, 128), f32),
            vmem((NX - 1, 16, 128), f32),
            vmem((NZ - 1, 16, 128), f32),
            dma((4,)),
            dma((22,)),
            dma((22,)),
            dma((N_BAND,)),
            dma((N_BAND,)),
            dma((N_BAND,)),
            dma((1,)),
            dma((7,)),
            dma((7,)),
            dma((NX - 1,)),
            dma((NX - 1,)),
            dma((NZ - 1,)),
            dma((NZ - 1,)),
        ],
        compiler_params=pltpu.CompilerParams(
            collective_id=0, has_side_effects=True, vmem_limit_bytes=40 * 1024 * 1024
        ),
        name="newton_step",
    )(
        given_load,
        displacement,
        mass_coef,
        stiffness,
        bearing_node.reshape(1, 4),
        stick_state.reshape(1, 4),
        slip_prev,
        bearing_old,
        bearing_weight.reshape(1, 4),
    )


def solution(mesh):
    return jax.shard_map(
        per_device,
        mesh=mesh,
        in_specs=(
            P(None, "sector", "band", None),
            P(None, "sector", "band", None),
            P("sector", "band", None),
            P("sector", "band", None),
            P(("sector", "band")),
            P(("sector", "band")),
            P(None, ("sector", "band")),
            P(None, ("sector", "band")),
            P(("sector", "band")),
        ),
        out_specs=(
            P(None, "sector", "band", None),
            P(None, "sector", "band", None),
            P(None, ("sector", "band")),
        ),
        check_vma=False,
    )
```

```python
import functools

import jax
import jax.numpy as jnp
from jax import lax
from jax.experimental import pallas as pl
from jax.experimental.pallas import tpu as pltpu
from jax.sharding import PartitionSpec as P

ITERS = 4
K_STICK = 4.0
K_VERT = 8.0
MU_FAST = 0.15
MU_SLOW = 0.04
RATE_GAIN = 2.0
RATE_DECAY = 2.0
V_FLOOR = 0.05
HIGHEST = lax.Precision.HIGHEST
MESH = pl.DeviceIdType.MESH

CA = 8
LAYERS = 16
NR = 256
DEPTH = 4
ROWS = CA + 2 * DEPTH
LEV = LAYERS + 2 * DEPTH
N_SECTOR = 64
N_BAND = 4
NX = 4
NZ = 8
PAIRS = [(0, 0), (0, 1), (1, 1), (0, 2), (1, 2), (2, 2), (0, 3), (1, 3), (2, 3), (3, 3), (0, 4), (1, 4), (2, 4), (3, 4)]


def coefficients(gram, e):
    def apply(d):
        q = [None] * 5

        def add(k, v):
            q[k] = v if q[k] is None else q[k] + v

        for j, dj in enumerate(d):
            t = e * dj
            add(j, t)
            if j == 0:
                add(1, t)
            else:
                add(j + 1, 0.5 * t)
                add(j - 1, 0.5 * t)
        return [v for v in q if v is not None]

    def inner(a, b):
        total = None
        for i, ai in enumerate(a):
            for j, bj in enumerate(b):
                term = ai * bj * gram(min(i, j), max(i, j))
                total = term if total is None else total + term
        return total

    def padded_add(a, b, scale):
        out = []
        for i in range(max(len(a), len(b))):
            if i >= len(a):
                out.append(scale * b[i])
            elif i >= len(b):
                out.append(a[i])
            else:
                out.append(a[i] + scale * b[i])
        return out

    one = jnp.ones_like(gram(0, 0))
    r, d, x = [one], [one], []
    rr = gram(0, 0)
    for k in range(ITERS):
        q = apply(d)
        alpha = rr / inner(d, q)
        x = padded_add(x, d, alpha)
        r = padded_add(r, q, -alpha)
        if k < ITERS - 1:
            new = inner(r, r)
            d = padded_add(r, d, new / rr)
            rr = new
    return x, r


def kernel(
    load_hbm,
    disp_hbm,
    mass_hbm,
    stiff_hbm,
    node_ref,
    stick_ref,
    slip_ref,
    old_ref,
    weight_ref,
    p,
    coef_ref,
    force_ref,
    st,
    me,
    u,
    k_row,
    k_up,
    k_dn,
    k_in,
    k_out,
    diag,
    bear,
    nodes,
    sticks,
    slips,
    olds,
    weighs,
    pack,
    packs,
    forces,
    force_in,
    early_a,
    early_b,
    late_a,
    late_b,
    load_sem,
    send_sem,
    recv_sem,
    pack_send,
    pack_recv,
    force_send,
    force_recv,
    ra_send,
    ra_recv,
    rb_send,
    rb_recv,
):
    s = lax.axis_index("sector")
    b = lax.axis_index("band")
    z, x, yh = s // 8, lax.rem(s // 2, 4), lax.rem(s, 2)
    s_dn, s_up = lax.rem(s + N_SECTOR - 1, N_SECTOR), lax.rem(s + 1, N_SECTOR)
    low, high = b == 0, b == N_BAND - 1

    group_a = []
    for da in range(2):
        for db in range(4):
            if (da, db) != (0, 0):
                group_a.append(((s // 2) * 2 + lax.rem(yh + da, 2), lax.rem(b + db, 4)))
    group_b = [
        ((lax.rem(z + i, NZ) * 4 + lax.rem(x + j, NX)) * 2 + yh, b)
        for i in range(NZ)
        for j in range(NX)
        if (i, j) != (0, 0)
    ]

    barrier = pltpu.get_barrier_semaphore()
    everyone = [(s_dn, b), (s_up, b)] + group_a + group_b
    for target in everyone:
        pl.semaphore_signal(barrier, inc=1, device_id=target, device_id_type=MESH)

    local = [
        pltpu.make_async_copy(stiff_hbm, st.at[0:CA, 0:LAYERS, :], load_sem.at[0]),
        pltpu.make_async_copy(disp_hbm, u.at[:, 0:CA, 0:LAYERS, :], load_sem.at[1]),
        pltpu.make_async_copy(mass_hbm, me.at[0:CA, 0:LAYERS, :], load_sem.at[2]),
        pltpu.make_async_copy(load_hbm, p.at[0, :, 0:CA, 0:LAYERS, :], load_sem.at[3]),
    ]
    small = [
        pltpu.make_async_copy(src, dst, load_sem.at[4 + n])
        for n, (src, dst) in enumerate(
            ((node_ref, nodes), (stick_ref, sticks), (slip_ref, slips), (old_ref, olds), (weight_ref, weighs))
        )
    ]
    for copy in local + small:
        copy.start()

    def remote(i, src, dst, target):
        return pltpu.make_async_remote_copy(
            src_ref=src,
            dst_ref=dst,
            send_sem=send_sem.at[i],
            recv_sem=recv_sem.at[i],
            device_id=target,
            device_id_type=MESH,
        )

    own, rim = slice(0, CA), slice(CA, ROWS)
    first, last = slice(0, DEPTH), slice(CA - DEPTH, CA)
    after, before = slice(CA, CA + DEPTH), slice(CA + DEPTH, ROWS)
    lay = slice(0, LAYERS)
    bottom, top = slice(0, DEPTH), slice(LAYERS - DEPTH, LAYERS)
    above, below = slice(LAYERS, LAYERS + DEPTH), slice(LAYERS + DEPTH, LEV)

    b_dn, b_up = (s, lax.rem(b + N_BAND - 1, N_BAND)), (s, lax.rem(b + 1, N_BAND))
    t_dn, t_up = (s_dn, b), (s_up, b)

    u_down = remote(8, disp_hbm.at[:, :, 0:1, :], u.at[:, own, LAYERS : LAYERS + 1, :], b_dn)
    u_up = remote(9, disp_hbm.at[:, :, LAYERS - 1 : LAYERS, :], u.at[:, own, LEV - 1 : LEV, :], b_up)
    st_down = remote(6, stiff_hbm.at[:, bottom, :], st.at[own, above, :], b_dn)
    st_up = remote(7, stiff_hbm.at[:, top, :], st.at[own, below, :], b_up)
    me_down = remote(10, mass_hbm.at[:, bottom, :], me.at[own, above, :], b_dn)
    me_up = remote(11, mass_hbm.at[:, top, :], me.at[own, below, :], b_up)
    st_first = remote(0, stiff_hbm.at[first], st.at[after, lay, :], t_dn)
    st_last = remote(1, stiff_hbm.at[last], st.at[before, lay, :], t_up)
    me_first = remote(2, mass_hbm.at[0 : DEPTH - 1], me.at[CA : CA + DEPTH - 1, lay, :], t_dn)
    me_last = remote(3, mass_hbm.at[CA - DEPTH + 1 : CA], me.at[CA + DEPTH + 1 : ROWS, lay, :], t_up)
    u_first = remote(4, disp_hbm.at[:, 0:1], u.at[:, CA : CA + 1, lay, :], t_dn)
    u_last = remote(5, disp_hbm.at[:, CA - 1 : CA], u.at[:, ROWS - 1 : ROWS, lay, :], t_up)
    st_rim_down = remote(12, st.at[rim, bottom, :], st.at[rim, above, :], b_dn)
    st_rim_up = remote(13, st.at[rim, top, :], st.at[rim, below, :], b_up)
    me_rim_down = remote(14, me.at[rim, bottom, :], me.at[rim, above, :], b_dn)
    me_rim_up = remote(15, me.at[rim, top, :], me.at[rim, below, :], b_up)
    bd_first = remote(16, bear.at[:, first, :], bear.at[:, after, :], t_dn)
    bd_last = remote(17, bear.at[:, last, :], bear.at[:, before, :], t_up)
    p_first = remote(18, p.at[0, :, first, lay, :], p.at[0, :, after, lay, :], t_dn)
    p_last = remote(19, p.at[0, :, last, lay, :], p.at[0, :, before, lay, :], t_up)
    p_down = remote(20, p.at[0, :, :, bottom, :], p.at[0, :, :, above, :], b_dn)
    p_up = remote(21, p.at[0, :, :, top, :], p.at[0, :, :, below, :], b_up)

    def pack_copy(slot):
        return pltpu.make_async_remote_copy(
            src_ref=pack,
            dst_ref=packs.at[slot],
            send_sem=pack_send.at[slot],
            recv_sem=pack_recv.at[slot],
            device_id=(s, 0),
            device_id_type=MESH,
        )

    def force_copy(slot):
        return pltpu.make_async_remote_copy(
            src_ref=forces.at[slot],
            dst_ref=force_in,
            send_sem=force_send.at[slot],
            recv_sem=force_recv.at[0],
            device_id=(s, slot),
            device_id_type=MESH,
        )

    def downward(*copies):
        @pl.when(jnp.logical_not(low))
        def _():
            for copy in copies:
                copy.start()

    def upward(*copies):
        @pl.when(jnp.logical_not(high))
        def _():
            for copy in copies:
                copy.start()

    def from_bands(downs, ups):
        @pl.when(jnp.logical_not(high))
        def _():
            for copy in downs:
                copy.wait_recv()

        @pl.when(jnp.logical_not(low))
        def _():
            for copy in ups:
                copy.wait_recv()

    pl.semaphore_wait(barrier, len(everyone))

    downward(u_down, st_down)
    upward(u_up, st_up)
    for copy in (u_first, u_last):
        copy.start()
    @pl.when(low)
    def _():
        st[:, LEV - DEPTH : LEV, :] = jnp.zeros((ROWS, DEPTH, NR), jnp.float32)
        me[:, LEV - DEPTH : LEV, :] = jnp.zeros((ROWS, DEPTH, NR), jnp.float32)
        u[:, 0:CA, LEV - 1 : LEV, :] = jnp.zeros((3, CA, 1, NR), jnp.float32)
        p[0, :, :, LEV - DEPTH : LEV, :] = jnp.zeros((3, ROWS, DEPTH, NR), jnp.float32)

    @pl.when(high)
    def _():
        st[:, LAYERS : LAYERS + DEPTH, :] = jnp.zeros((ROWS, DEPTH, NR), jnp.float32)
        me[:, LAYERS : LAYERS + DEPTH, :] = jnp.zeros((ROWS, DEPTH, NR), jnp.float32)
        u[:, 0:CA, LAYERS : LAYERS + 1, :] = jnp.zeros((3, CA, 1, NR), jnp.float32)
        p[0, :, :, LAYERS : LAYERS + DEPTH, :] = jnp.zeros((3, ROWS, DEPTH, NR), jnp.float32)

    def face(a, c, scale=1.0):
        return (2.0 * scale) * a * c / jnp.maximum(a + c, 0.25)

    def spread_to(group, slots, which, send, recv):
        n = len(group)
        return [
            pltpu.make_async_remote_copy(
                src_ref=slots.at[n : n + 1, :],
                dst_ref=slots.at[k : k + 1, :],
                send_sem=send.at[which, k],
                recv_sem=recv.at[which, k],
                device_id=target,
                device_id_type=MESH,
            )
            for k, target in enumerate(group)
        ]

    def send_row(row, group, slots, which, send, recv):
        slots[len(group) : len(group) + 1, :] = row
        copies = spread_to(group, slots, which, send, recv)
        for copy in copies:
            copy.start()
        return copies

    def received(copies, slots):
        for copy in copies:
            copy.wait()
        return jnp.sum(slots[...], axis=0, keepdims=True)

    local[0].wait()
    local[2].wait()
    k_row[0, lay, :] = face(st[0, lay, :], st[1, lay, :])

    def powers_of(i, total):
        k = face(st[i, lay, :], st[i + 1, lay, :])
        d = me[i, lay, :] + 6.0 * (k + k_row[i - 1, lay, :])
        k_row[i, lay, :] = k
        d = d * d
        d = d * d
        return total + d * d

    powers = lax.fori_loop(1, CA - 1, powers_of, jnp.zeros((LAYERS, NR), jnp.float32), unroll=True)
    total = jnp.sum(jnp.sum(powers, axis=0, keepdims=True), axis=1, keepdims=True)
    sent = send_row(jnp.broadcast_to(total, (1, 128)), group_a, early_a, 0, ra_send, ra_recv)
    for copy in (st_first, st_last):
        copy.start()
    downward(me_down)
    upward(me_up)
    pack[...] = jnp.zeros_like(pack)
    me[CA + DEPTH - 1 : CA + DEPTH + 1, lay, :] = jnp.zeros((2, LAYERS, NR), jnp.float32)
    for copy in small:
        copy.wait()
    pack[0:1, 0:4] = nodes[...].astype(jnp.float32)
    pack[1:2, 0:4] = sticks[...].astype(jnp.float32)
    pack[2:4, 0:4] = slips[...]
    pack[4:6, 0:4] = olds[...]
    pack[6:7, 0:4] = weighs[...]

    for slot in range(1, N_BAND):

        @pl.when(b == slot)
        def _():
            pack_copy(slot).start()


    lane = lax.broadcasted_iota(jnp.int32, (LEV, NR), 1)

    def conductances_of(i, scale=1.0):
        a = st[i]
        ku = face(a, pltpu.roll(a, LEV - 1, 0), scale)
        ko = jnp.where(lane == NR - 1, 0.0, face(a, pltpu.roll(a, NR - 1, 1), scale))
        k_up[i] = ku
        k_dn[i] = pltpu.roll(ku, 1, 0)
        k_out[i] = ko
        k_in[i] = pltpu.roll(ko, 1, 1)

    from_bands([u_down, st_down], [u_up, st_up])

    @pl.loop(0, CA)
    def _(i):
        conductances_of(i)

    local[1].wait()
    local[3].wait()

    gains = (1.0, 1.0, 2.0)

    @pl.loop(0, CA)
    def _(i):
        up, dn = jnp.minimum(i + 1, CA - 1), jnp.maximum(i - 1, 0)
        kr_up = k_row[jnp.minimum(i, CA - 2), lay, :]
        kr_dn = k_row[dn, lay, :]
        ku, kd, ko, ki = k_up[i, lay, :], k_dn[i, lay, :], k_out[i, lay, :], k_in[i, lay, :]
        m = me[i, lay, :]
        for c in range(3):
            whole = u[c, i]
            v = whole[0:LAYERS]
            above_v = pltpu.roll(whole, LEV - 1, 0)[0:LAYERS]
            below_v = pltpu.roll(whole, 1, 0)[0:LAYERS]
            acc = ku * (above_v - v) + kd * (below_v - v)
            acc = acc + ko * (pltpu.roll(v, NR - 1, 1) - v) + ki * (pltpu.roll(v, 1, 1) - v)
            acc = acc + kr_up * (u[c, up, lay, :] - v) + kr_dn * (u[c, dn, lay, :] - v)
            p[0, c, i, lay, :] = p[0, c, i, lay, :] - m * v + gains[c] * acc
    for copy in (p_first, p_last, me_first, me_last):
        copy.start()
    sent = send_row(received(sent, early_a), group_b, early_b, 0, rb_send, rb_recv)

    @pl.when(low)
    def _():
        packs[0] = pack[...]
        for slot in range(1, N_BAND):
            pack_copy(slot).wait_recv()
        t = packs[0]
        for slot in range(1, N_BAND):
            t = t + pltpu.roll(packs[slot], 4 * slot, 1)
        t = t[:, 0:128]
        node = t[0:1, :].astype(jnp.int32)
        stick = t[1:2, :] > 0.5
        row_of = node // NR
        col_of = lax.rem(node, NR)
        real = lax.broadcasted_iota(jnp.int32, (1, 128), 1) < 4 * N_BAND
        col_hot = jnp.where(
            jnp.logical_and(lax.broadcasted_iota(jnp.int32, (NR, 128), 0) == col_of, real), 1.0, 0.0
        ).astype(jnp.float32)
        row_hot = jnp.where(lax.broadcasted_iota(jnp.int32, (CA, 128), 0) == row_of, 1.0, 0.0).astype(jnp.float32)
        raft = jnp.concatenate([u[c, r, 0:1, :] for c in range(3) for r in range(CA)], axis=0)
        picked = jnp.dot(raft, col_hot, precision=HIGHEST, preferred_element_type=jnp.float32)
        at = [jnp.sum(picked[CA * c : CA * (c + 1)] * row_hot, axis=0, keepdims=True) for c in range(3)]
        trial = [K_STICK * (at[c] - t[2 + c : 3 + c]) for c in range(2)]
        rate = [RATE_GAIN * (at[c] - t[4 + c : 5 + c]) for c in range(2)]
        speed = jnp.sqrt(rate[0] * rate[0] + rate[1] * rate[1] + V_FLOOR * V_FLOOR)
        friction = MU_FAST - (MU_FAST - MU_SLOW) * jnp.exp(-RATE_DECAY * speed)
        capacity = friction * t[6:7]
        magnitude = jnp.sqrt(trial[0] * trial[0] + trial[1] * trial[1])
        largest = jnp.maximum(magnitude, capacity)
        largest = jnp.where(real, largest, 1.0)
        force = [jnp.where(stick, trial[c], capacity * trial[c] / largest) for c in range(2)]
        force = [jnp.where(real, f, 0.0) for f in force + [K_VERT * at[2]]]
        stick_k = jnp.where(jnp.logical_and(stick, real), K_STICK, 0.0)
        vert_k = jnp.where(real, K_VERT, 0.0)
        weights = jnp.concatenate([row_hot * v for v in force + [stick_k, vert_k]], axis=0)
        spread = lax.dot_general(
            weights, col_hot, (((1,), (1,)), ((), ())), precision=HIGHEST, preferred_element_type=jnp.float32
        )
        for n in range(5):
            bear[n, 0:CA] = spread[CA * n : CA * (n + 1)]
        tile = jnp.concatenate(force + [jnp.zeros((5, 128), jnp.float32)], axis=0)
        force_in[...] = tile
        for slot in range(1, N_BAND):
            forces[slot] = pltpu.roll(tile, 128 - 4 * slot, 1)
        for slot in range(1, N_BAND):
            force_copy(slot).start()

    @pl.when(jnp.logical_not(low))
    def _():
        bear[:, 0:CA, :] = jnp.zeros((5, CA, NR), jnp.float32)

    bd_first.start()
    bd_last.start()


    for copy in (st_first, st_last):
        copy.wait_recv()
    downward(st_rim_down)
    upward(st_rim_up)

    for copy in (u_first, u_last):
        copy.wait_recv()
    for copy in (p_first, p_last):
        copy.wait_send()
    for copy in (p_first, p_last):
        copy.wait_recv()
    for here, there in ((CA - 1, CA), (0, ROWS - 1)):
        k = face(st[here, lay, :], st[there, lay, :])
        for c in range(3):
            flux = gains[c] * k * (u[c, there, lay, :] - u[c, here, lay, :])
            p[0, c, here, lay, :] = p[0, c, here, lay, :] + flux
            p[0, c, there, lay, :] = p[0, c, there, lay, :] - flux
    downward(p_down)
    upward(p_up)
    for copy in (me_first, me_last):
        copy.wait_recv()
    downward(me_rim_down)
    upward(me_rim_up)

    mean = received(sent, early_b) * (1.0 / (N_SECTOR * N_BAND * (CA - 2) * LAYERS * NR))
    e128 = jnp.sqrt(jnp.sqrt(jnp.sqrt(mean)))
    scale128 = 2.0 / e128
    scale = jnp.concatenate([scale128, scale128], axis=1)
    from_bands([st_rim_down], [st_rim_up])
    lev = lax.broadcasted_iota(jnp.int32, (LEV, NR), 0)

    @pl.loop(0, ROWS)
    def _(i):
        conductances_of(i, scale)
        k_row[i] = face(st[i], st[lax.rem(i + 1, ROWS)], scale)

    for copy in (bd_first, bd_last):
        copy.wait_recv()

    @pl.when(low)
    def _():
        for c in range(3):
            for i in range(ROWS):
                p[0, c, i, 0:1, :] = p[0, c, i, 0:1, :] - bear[c, i : i + 1, :]

    from_bands([me_down, me_rim_down], [me_up, me_rim_up])

    @pl.loop(0, ROWS)
    def _(i):
        near = k_up[i] + k_dn[i] + k_out[i] + k_in[i] + k_row[i] + k_row[lax.rem(i + ROWS - 1, ROWS)]
        base = scale * me[i] - 2.0
        for h in range(2):
            extra = scale * bear[3 + h, pl.ds(i, 1), :]
            diag[h, i] = base + (h + 1.0) * near + jnp.where(lev == 0, extra, 0.0)

    from_bands([p_down], [p_up])

    sums = {}

    def one_row(j, i, tall=slice(0, LEV)):
        up, dn = lax.rem(i + 1, ROWS), lax.rem(i + ROWS - 1, ROWS)
        kr_up, kr_dn, ku, kd, ko, ki = [
            k[n, tall, :] for k, n in ((k_row, i), (k_row, dn), (k_up, i), (k_dn, i), (k_out, i), (k_in, i))
        ]
        out = []
        for c in range(3):
            whole = p[j, c, i]
            v = whole[tall]
            near = ku * pltpu.roll(whole, LEV - 1, 0)[tall] + kd * pltpu.roll(whole, 1, 0)[tall]
            near = near + ko * pltpu.roll(v, NR - 1, 1) + ki * pltpu.roll(v, 1, 1)
            near = near + kr_up * p[j, c, up, tall, :] + kr_dn * p[j, c, dn, tall, :]
            if c == 2:
                near = near + near
            w = diag[c // 2, i, tall, :] * v - near
            w = 0.5 * w if j == 0 else w - p[j - 1, c, i, tall, :]
            p[j + 1, c, i, tall, :] = w
            out.append(w)
        return out

    for j in range(ITERS):
        pairs = [q for q in PAIRS if q[1] == j + 1 or (j == 0 and q == (0, 0))]

        def own_row(i, acc):
            new = one_row(j, i, lay if j == ITERS - 1 else slice(0, LEV))
            acc = list(acc)
            for c in range(3):
                w = new[c][0:LAYERS]
                for n, (lo, hi) in enumerate(pairs):
                    a = w if lo == j + 1 else p[lo, c, i, lay, :]
                    d = w if hi == j + 1 else p[hi, c, i, lay, :]
                    acc[n] = acc[n] + a * d
            return tuple(acc)

        totals = lax.fori_loop(0, CA, own_row, tuple(jnp.zeros((LAYERS, NR), jnp.float32) for _ in pairs), unroll=2)
        sums.update(zip(pairs, totals))
        wide = ITERS - 1 - j
        if wide:

            @pl.loop(0, 2 * wide, unroll=2)
            def _(i):
                one_row(j, jnp.where(i < wide, CA + i, ROWS - 1 - (i - wide)))

    rows = []
    for q in PAIRS:
        t = jnp.sum(sums[q], axis=0, keepdims=True)
        rows.append(t[:, 0:128] + t[:, 128:256])
    rows = jnp.concatenate(rows + [jnp.zeros((16 - len(PAIRS), 128), jnp.float32)], axis=0)
    eye = lax.broadcasted_iota(jnp.int32, (16, 128), 0) == lax.broadcasted_iota(jnp.int32, (16, 128), 1)
    row = jnp.sum(jnp.where(eye, jnp.sum(rows, axis=1, keepdims=True), 0.0), axis=0, keepdims=True)
    row = received(send_row(row, group_a, late_a, 1, ra_send, ra_recv), late_a)
    row = received(send_row(row, group_b, late_b, 1, rb_send, rb_recv), late_b)
    g = jnp.broadcast_to(jnp.sum(jnp.where(eye, row, 0.0), axis=1, keepdims=True), (16, 128))
    where = {q: n for n, q in enumerate(PAIRS)}
    grams = {q: g[where[q] : where[q] + 1, :] for q in PAIRS}
    xs, rs = coefficients(lambda i, j: grams[(i, j)], e128)
    for n, v in enumerate(xs + rs):
        coef_ref[n : n + 1, :] = v

    @pl.when(jnp.logical_not(low))
    def _():
        force_copy(1).wait_recv()

    force_ref[...] = force_in[...]

    for slot in range(1, N_BAND):

        @pl.when(b == slot)
        def _():
            pack_copy(slot).wait_send()

    @pl.when(low)
    def _():
        for slot in range(1, N_BAND):
            force_copy(slot).wait_send()

    for copy in (st_first, st_last, u_first, u_last, me_first, me_last, bd_first, bd_last):
        copy.wait_send()

    @pl.when(jnp.logical_not(low))
    def _():
        for copy in (u_down, st_down, me_down, st_rim_down, me_rim_down, p_down):
            copy.wait_send()

    @pl.when(jnp.logical_not(high))
    def _():
        for copy in (u_up, st_up, me_up, st_rim_up, me_rim_up, p_up):
            copy.wait_send()


def combine(p, coef, force, inc_hbm, res_hbm, force_hbm, inc, res, out, sems):
    out[...] = force[0:3, 0:4]
    copies = [pltpu.make_async_copy(out, force_hbm, sems.at[0])]
    copies[0].start()
    rows = [jnp.concatenate([coef[n : n + 1, :]] * 2, axis=1) for n in range(2 * ITERS + 1)]
    xs, rs = rows[:ITERS], rows[ITERS:]
    step = CA // 4
    for chunk in range(4):
        span = slice(chunk * step, (chunk + 1) * step)
        for i in range(chunk * step, (chunk + 1) * step):
            for c in range(3):
                vs = [p[j, c, i, 0:LAYERS, :] for j in range(ITERS + 1)]
                a, r = xs[0] * vs[0], rs[0] * vs[0]
                for j in range(1, ITERS):
                    a = a + xs[j] * vs[j]
                for j in range(1, ITERS + 1):
                    r = r + rs[j] * vs[j]
                inc[c, i] = a
                res[c, i] = r
        for n, (src, dst) in enumerate(((inc, inc_hbm), (res, res_hbm))):
            copy = pltpu.make_async_copy(src.at[:, span], dst.at[:, span], sems.at[1 + 2 * chunk + n])
            copy.start()
            copies.append(copy)
    for copy in copies:
        copy.wait()


def per_device(
    given_load,
    displacement,
    mass_coef,
    stiffness,
    bearing_node,
    stick_state,
    slip_prev,
    bearing_old,
    bearing_weight,
):
    f32, i32 = jnp.float32, jnp.int32
    vmem, dma = pltpu.VMEM, pltpu.SemaphoreType.DMA
    field = jax.ShapeDtypeStruct((3, CA, LAYERS, NR), f32)
    in_vmem = pl.BlockSpec(memory_space=vmem)
    in_hbm = pl.BlockSpec(memory_space=pltpu.HBM)
    basis, coef, force = pl.pallas_call(
        kernel,
        out_shape=(
            jax.ShapeDtypeStruct((ITERS + 1, 3, ROWS, LEV, NR), f32),
            jax.ShapeDtypeStruct((16, 128), f32),
            jax.ShapeDtypeStruct((8, 128), f32),
        ),
        in_specs=[in_hbm] * 9,
        out_specs=(in_vmem, in_vmem, in_vmem),
        scratch_shapes=[
            vmem((ROWS, LEV, NR), f32),
            vmem((ROWS, LEV, NR), f32),
            vmem((3, ROWS, LEV, NR), f32),
            vmem((ROWS, LEV, NR), f32),
            vmem((ROWS, LEV, NR), f32),
            vmem((ROWS, LEV, NR), f32),
            vmem((ROWS, LEV, NR), f32),
            vmem((ROWS, LEV, NR), f32),
            vmem((2, ROWS, LEV, NR), f32),
            vmem((5, ROWS, NR), f32),
            vmem((1, 4), i32),
            vmem((1, 4), i32),
            vmem((2, 4), f32),
            vmem((2, 4), f32),
            vmem((1, 4), f32),
            vmem((8, 128), f32),
            vmem((N_BAND, 8, 128), f32),
            vmem((N_BAND, 8, 128), f32),
            vmem((8, 128), f32),
            vmem((8, 128), f32),
            vmem((32, 128), f32),
            vmem((8, 128), f32),
            vmem((32, 128), f32),
            dma((9,)),
            dma((22,)),
            dma((22,)),
            dma((N_BAND,)),
            dma((N_BAND,)),
            dma((N_BAND,)),
            dma((1,)),
            dma((2, 7)),
            dma((2, 7)),
            dma((2, 31)),
            dma((2, 31)),
        ],
        compiler_params=pltpu.CompilerParams(
            collective_id=0, has_side_effects=True, vmem_limit_bytes=32 * 1024 * 1024
        ),
        name="newton_step",
    )(
        *[
            pltpu.with_memory_space_constraint(a, pltpu.HBM)
            for a in (
                given_load,
                displacement,
                mass_coef,
                stiffness,
                bearing_node.reshape(1, 4),
                stick_state.reshape(1, 4),
                slip_prev,
                bearing_old,
                bearing_weight.reshape(1, 4),
            )
        ]
    )
    return pl.pallas_call(
        combine,
        out_shape=(field, field, jax.ShapeDtypeStruct((3, 4), f32)),
        in_specs=[in_vmem] * 3,
        out_specs=(in_hbm, in_hbm, in_hbm),
        scratch_shapes=[
            vmem((3, CA, LAYERS, NR), f32),
            vmem((3, CA, LAYERS, NR), f32),
            vmem((3, 4), f32),
            dma((9,)),
        ],
        compiler_params=pltpu.CompilerParams(vmem_limit_bytes=16 * 1024 * 1024),
        name="combine",
    )(basis, coef, force)


def solution(mesh):
    return jax.shard_map(
        per_device,
        mesh=mesh,
        in_specs=(
            P(None, "sector", "band", None),
            P(None, "sector", "band", None),
            P("sector", "band", None),
            P("sector", "band", None),
            P(("sector", "band")),
            P(("sector", "band")),
            P(None, ("sector", "band")),
            P(None, ("sector", "band")),
            P(("sector", "band")),
        ),
        out_specs=(
            P(None, "sector", "band", None),
            P(None, "sector", "band", None),
            P(None, ("sector", "band")),
        ),
        check_vma=False,
    )
```

```python
import functools

import jax
import jax.numpy as jnp
from jax import lax
from jax.experimental import pallas as pl
from jax.experimental.pallas import tpu as pltpu
from jax.sharding import PartitionSpec as P

ITERS = 4
K_STICK = 4.0
K_VERT = 8.0
MU_FAST = 0.15
MU_SLOW = 0.04
RATE_GAIN = 2.0
RATE_DECAY = 2.0
V_FLOOR = 0.05
HIGHEST = lax.Precision.HIGHEST
MESH = pl.DeviceIdType.MESH

CA = 8
LAYERS = 16
NR = 256
DEPTH = 4
ROWS = CA + 2 * DEPTH
LEV = LAYERS + 2 * DEPTH
N_SECTOR = 64
N_BAND = 4
NX = 4
NZ = 8
PAIRS = [(0, 0), (0, 1), (1, 1), (0, 2), (1, 2), (2, 2), (0, 3), (1, 3), (2, 3), (3, 3), (0, 4), (1, 4), (2, 4), (3, 4)]


def coefficients(gram, e):
    def apply(d):
        q = [None] * 5

        def add(k, v):
            q[k] = v if q[k] is None else q[k] + v

        for j, dj in enumerate(d):
            t = e * dj
            add(j, t)
            if j == 0:
                add(1, t)
            else:
                add(j + 1, 0.5 * t)
                add(j - 1, 0.5 * t)
        return [v for v in q if v is not None]

    def inner(a, b):
        total = None
        for i, ai in enumerate(a):
            for j, bj in enumerate(b):
                term = ai * bj * gram(min(i, j), max(i, j))
                total = term if total is None else total + term
        return total

    def padded_add(a, b, scale):
        out = []
        for i in range(max(len(a), len(b))):
            if i >= len(a):
                out.append(scale * b[i])
            elif i >= len(b):
                out.append(a[i])
            else:
                out.append(a[i] + scale * b[i])
        return out

    one = jnp.ones_like(gram(0, 0))
    r, d, x = [one], [one], []
    rr = gram(0, 0)
    for k in range(ITERS):
        q = apply(d)
        alpha = rr / inner(d, q)
        x = padded_add(x, d, alpha)
        r = padded_add(r, q, -alpha)
        if k < ITERS - 1:
            new = inner(r, r)
            d = padded_add(r, d, new / rr)
            rr = new
    return x, r


def kernel(
    load_hbm,
    disp_hbm,
    mass_hbm,
    stiff_hbm,
    node_ref,
    stick_ref,
    slip_ref,
    old_ref,
    weight_ref,
    p,
    coef_ref,
    force_ref,
    st,
    me,
    u,
    k_row,
    k_up,
    k_dn,
    k_in,
    k_out,
    diag,
    bear,
    nodes,
    sticks,
    slips,
    olds,
    weighs,
    pack,
    packs,
    forces,
    force_in,
    early_a,
    early_b,
    late_a,
    late_b,
    load_sem,
    send_sem,
    recv_sem,
    pack_send,
    pack_recv,
    force_send,
    force_recv,
    red_sem,
):
    s = lax.axis_index("sector")
    b = lax.axis_index("band")
    z, x, yh = s // 8, lax.rem(s // 2, 4), lax.rem(s, 2)
    s_dn, s_up = lax.rem(s + N_SECTOR - 1, N_SECTOR), lax.rem(s + 1, N_SECTOR)
    low, high = b == 0, b == N_BAND - 1

    def group_a(n):
        k = n + 1
        return ((s // 2) * 2 + lax.rem(yh + k // N_BAND, 2), lax.rem(b + lax.rem(k, N_BAND), N_BAND))

    def group_b(n):
        k = n + 1
        return ((lax.rem(z + k // NX, NZ) * NX + lax.rem(x + lax.rem(k, NX), NX)) * 2 + yh, b)

    size_a, size_b = 2 * N_BAND - 1, NZ * NX - 1

    barrier = pltpu.get_barrier_semaphore()
    for target in ((s_dn, b), (s_up, b)):
        pl.semaphore_signal(barrier, inc=1, device_id=target, device_id_type=MESH)
    for group, size in ((group_a, size_a), (group_b, size_b)):

        @pl.loop(0, size)
        def _(n):
            pl.semaphore_signal(barrier, inc=1, device_id=group(n), device_id_type=MESH)

    local = [
        pltpu.make_async_copy(stiff_hbm, st.at[0:CA, 0:LAYERS, :], load_sem.at[0]),
        pltpu.make_async_copy(disp_hbm, u.at[:, 0:CA, 0:LAYERS, :], load_sem.at[1]),
        pltpu.make_async_copy(mass_hbm, me.at[0:CA, 0:LAYERS, :], load_sem.at[2]),
        pltpu.make_async_copy(load_hbm, p.at[0, :, 0:CA, 0:LAYERS, :], load_sem.at[3]),
    ]
    small = [
        pltpu.make_async_copy(src, dst, load_sem.at[4 + n])
        for n, (src, dst) in enumerate(
            ((node_ref, nodes), (stick_ref, sticks), (slip_ref, slips), (old_ref, olds), (weight_ref, weighs))
        )
    ]
    for copy in local + small:
        copy.start()

    def remote(i, src, dst, target):
        return pltpu.make_async_remote_copy(
            src_ref=src,
            dst_ref=dst,
            send_sem=send_sem.at[i],
            recv_sem=recv_sem.at[i],
            device_id=target,
            device_id_type=MESH,
        )

    own, rim = slice(0, CA), slice(CA, ROWS)
    first, last = slice(0, DEPTH), slice(CA - DEPTH, CA)
    after, before = slice(CA, CA + DEPTH), slice(CA + DEPTH, ROWS)
    lay = slice(0, LAYERS)
    bottom, top = slice(0, DEPTH), slice(LAYERS - DEPTH, LAYERS)
    above, below = slice(LAYERS, LAYERS + DEPTH), slice(LAYERS + DEPTH, LEV)

    b_dn, b_up = (s, lax.rem(b + N_BAND - 1, N_BAND)), (s, lax.rem(b + 1, N_BAND))
    t_dn, t_up = (s_dn, b), (s_up, b)

    u_down = remote(8, disp_hbm.at[:, :, 0:1, :], u.at[:, own, LAYERS : LAYERS + 1, :], b_dn)
    u_up = remote(9, disp_hbm.at[:, :, LAYERS - 1 : LAYERS, :], u.at[:, own, LEV - 1 : LEV, :], b_up)
    st_down = remote(6, stiff_hbm.at[:, bottom, :], st.at[own, above, :], b_dn)
    st_up = remote(7, stiff_hbm.at[:, top, :], st.at[own, below, :], b_up)
    me_down = remote(10, mass_hbm.at[:, bottom, :], me.at[own, above, :], b_dn)
    me_up = remote(11, mass_hbm.at[:, top, :], me.at[own, below, :], b_up)
    st_first = remote(0, stiff_hbm.at[first], st.at[after, lay, :], t_dn)
    st_last = remote(1, stiff_hbm.at[last], st.at[before, lay, :], t_up)
    me_first = remote(2, mass_hbm.at[0 : DEPTH - 1], me.at[CA : CA + DEPTH - 1, lay, :], t_dn)
    me_last = remote(3, mass_hbm.at[CA - DEPTH + 1 : CA], me.at[CA + DEPTH + 1 : ROWS, lay, :], t_up)
    u_first = remote(4, disp_hbm.at[:, 0:1], u.at[:, CA : CA + 1, lay, :], t_dn)
    u_last = remote(5, disp_hbm.at[:, CA - 1 : CA], u.at[:, ROWS - 1 : ROWS, lay, :], t_up)
    st_rim_down = remote(12, st.at[rim, bottom, :], st.at[rim, above, :], b_dn)
    st_rim_up = remote(13, st.at[rim, top, :], st.at[rim, below, :], b_up)
    me_rim_down = remote(14, me.at[rim, bottom, :], me.at[rim, above, :], b_dn)
    me_rim_up = remote(15, me.at[rim, top, :], me.at[rim, below, :], b_up)
    bd_first = remote(16, bear.at[:, first, :], bear.at[:, after, :], t_dn)
    bd_last = remote(17, bear.at[:, last, :], bear.at[:, before, :], t_up)
    p_first = remote(18, p.at[0, :, first, lay, :], p.at[0, :, after, lay, :], t_dn)
    p_last = remote(19, p.at[0, :, last, lay, :], p.at[0, :, before, lay, :], t_up)
    p_down = remote(20, p.at[0, :, :, bottom, :], p.at[0, :, :, above, :], b_dn)
    p_up = remote(21, p.at[0, :, :, top, :], p.at[0, :, :, below, :], b_up)

    def pack_copy(slot):
        return pltpu.make_async_remote_copy(
            src_ref=pack,
            dst_ref=packs.at[slot],
            send_sem=pack_send.at[slot],
            recv_sem=pack_recv.at[slot],
            device_id=(s, 0),
            device_id_type=MESH,
        )

    def force_copy(slot):
        return pltpu.make_async_remote_copy(
            src_ref=forces.at[slot],
            dst_ref=force_in,
            send_sem=force_send.at[slot],
            recv_sem=force_recv.at[0],
            device_id=(s, slot),
            device_id_type=MESH,
        )

    def downward(*copies):
        @pl.when(jnp.logical_not(low))
        def _():
            for copy in copies:
                copy.start()

    def upward(*copies):
        @pl.when(jnp.logical_not(high))
        def _():
            for copy in copies:
                copy.start()

    def from_bands(downs, ups):
        @pl.when(jnp.logical_not(high))
        def _():
            for copy in downs:
                copy.wait_recv()

        @pl.when(jnp.logical_not(low))
        def _():
            for copy in ups:
                copy.wait_recv()

    pl.semaphore_wait(barrier, 2 + size_a + size_b)

    downward(u_down, st_down)
    upward(u_up, st_up)
    for copy in (u_first, u_last):
        copy.start()
    @pl.when(low)
    def _():
        st[:, LEV - DEPTH : LEV, :] = jnp.zeros((ROWS, DEPTH, NR), jnp.float32)
        me[:, LEV - DEPTH : LEV, :] = jnp.zeros((ROWS, DEPTH, NR), jnp.float32)
        u[:, 0:CA, LEV - 1 : LEV, :] = jnp.zeros((3, CA, 1, NR), jnp.float32)
        p[0, :, :, LEV - DEPTH : LEV, :] = jnp.zeros((3, ROWS, DEPTH, NR), jnp.float32)

    @pl.when(high)
    def _():
        st[:, LAYERS : LAYERS + DEPTH, :] = jnp.zeros((ROWS, DEPTH, NR), jnp.float32)
        me[:, LAYERS : LAYERS + DEPTH, :] = jnp.zeros((ROWS, DEPTH, NR), jnp.float32)
        u[:, 0:CA, LAYERS : LAYERS + 1, :] = jnp.zeros((3, CA, 1, NR), jnp.float32)
        p[0, :, :, LAYERS : LAYERS + DEPTH, :] = jnp.zeros((3, ROWS, DEPTH, NR), jnp.float32)

    def face(a, c, scale=1.0):
        return (2.0 * scale) * a * c / jnp.maximum(a + c, 0.25)

    def send_row(row, group, slots, send, recv):
        n_others = slots.shape[0] - 1
        slots[n_others] = row

        @pl.loop(0, n_others)
        def _(n):
            pltpu.make_async_remote_copy(
                src_ref=slots.at[n_others],
                dst_ref=slots.at[n],
                send_sem=send,
                recv_sem=recv,
                device_id=group(n),
                device_id_type=MESH,
            ).start()

    def received(slots, send, recv):
        others = slots.at[0 : slots.shape[0] - 1]
        pltpu.make_async_copy(others, others, recv).wait()
        pltpu.make_async_copy(others, others, send).wait()
        return jnp.sum(slots[...], axis=0)

    local[0].wait()
    local[2].wait()
    k_row[0, lay, :] = face(st[0, lay, :], st[1, lay, :])

    def powers_of(i, total):
        k = face(st[i, lay, :], st[i + 1, lay, :])
        d = me[i, lay, :] + 6.0 * (k + k_row[i - 1, lay, :])
        k_row[i, lay, :] = k
        d = d * d
        d = d * d
        return total + d * d

    powers = lax.fori_loop(1, CA - 1, powers_of, jnp.zeros((LAYERS, NR), jnp.float32), unroll=True)
    total = jnp.sum(jnp.sum(powers, axis=0, keepdims=True), axis=1, keepdims=True)
    send_row(jnp.broadcast_to(total, (1, 128)), group_a, early_a, red_sem.at[0], red_sem.at[1])
    for copy in (st_first, st_last):
        copy.start()
    downward(me_down)
    upward(me_up)
    pack[...] = jnp.zeros_like(pack)
    me[CA + DEPTH - 1 : CA + DEPTH + 1, lay, :] = jnp.zeros((2, LAYERS, NR), jnp.float32)
    for copy in small:
        copy.wait()
    pack[0:1, 0:4] = nodes[...].astype(jnp.float32)
    pack[1:2, 0:4] = sticks[...].astype(jnp.float32)
    pack[2:4, 0:4] = slips[...]
    pack[4:6, 0:4] = olds[...]
    pack[6:7, 0:4] = weighs[...]

    for slot in range(1, N_BAND):

        @pl.when(b == slot)
        def _():
            pack_copy(slot).start()


    lane = lax.broadcasted_iota(jnp.int32, (LEV, NR), 1)

    def conductances_of(i, scale=1.0):
        a = st[i]
        ku = face(a, pltpu.roll(a, LEV - 1, 0), scale)
        ko = jnp.where(lane == NR - 1, 0.0, face(a, pltpu.roll(a, NR - 1, 1), scale))
        k_up[i] = ku
        k_dn[i] = pltpu.roll(ku, 1, 0)
        k_out[i] = ko
        k_in[i] = pltpu.roll(ko, 1, 1)

    from_bands([u_down, st_down], [u_up, st_up])

    @pl.loop(0, CA)
    def _(i):
        conductances_of(i)

    local[1].wait()
    local[3].wait()

    gains = (1.0, 1.0, 2.0)

    @pl.loop(0, CA)
    def _(i):
        up, dn = jnp.minimum(i + 1, CA - 1), jnp.maximum(i - 1, 0)
        kr_up = k_row[jnp.minimum(i, CA - 2), lay, :]
        kr_dn = k_row[dn, lay, :]
        ku, kd, ko, ki = k_up[i, lay, :], k_dn[i, lay, :], k_out[i, lay, :], k_in[i, lay, :]
        m = me[i, lay, :]
        for c in range(3):
            whole = u[c, i]
            v = whole[0:LAYERS]
            above_v = pltpu.roll(whole, LEV - 1, 0)[0:LAYERS]
            below_v = pltpu.roll(whole, 1, 0)[0:LAYERS]
            acc = ku * (above_v - v) + kd * (below_v - v)
            acc = acc + ko * (pltpu.roll(v, NR - 1, 1) - v) + ki * (pltpu.roll(v, 1, 1) - v)
            acc = acc + kr_up * (u[c, up, lay, :] - v) + kr_dn * (u[c, dn, lay, :] - v)
            p[0, c, i, lay, :] = p[0, c, i, lay, :] - m * v + gains[c] * acc
    for copy in (p_first, p_last, me_first, me_last):
        copy.start()
    send_row(received(early_a, red_sem.at[0], red_sem.at[1]), group_b, early_b, red_sem.at[2], red_sem.at[3])

    @pl.when(low)
    def _():
        packs[0] = pack[...]
        for slot in range(1, N_BAND):
            pack_copy(slot).wait_recv()
        t = packs[0]
        for slot in range(1, N_BAND):
            t = t + pltpu.roll(packs[slot], 4 * slot, 1)
        t = t[:, 0:128]
        node = t[0:1, :].astype(jnp.int32)
        stick = t[1:2, :] > 0.5
        row_of = node // NR
        col_of = lax.rem(node, NR)
        real = lax.broadcasted_iota(jnp.int32, (1, 128), 1) < 4 * N_BAND
        col_hot = jnp.where(
            jnp.logical_and(lax.broadcasted_iota(jnp.int32, (NR, 128), 0) == col_of, real), 1.0, 0.0
        ).astype(jnp.float32)
        row_hot = jnp.where(lax.broadcasted_iota(jnp.int32, (CA, 128), 0) == row_of, 1.0, 0.0).astype(jnp.float32)
        raft = jnp.concatenate([u[c, r, 0:1, :] for c in range(3) for r in range(CA)], axis=0)
        picked = jnp.dot(raft, col_hot, precision=HIGHEST, preferred_element_type=jnp.float32)
        at = [jnp.sum(picked[CA * c : CA * (c + 1)] * row_hot, axis=0, keepdims=True) for c in range(3)]
        trial = [K_STICK * (at[c] - t[2 + c : 3 + c]) for c in range(2)]
        rate = [RATE_GAIN * (at[c] - t[4 + c : 5 + c]) for c in range(2)]
        speed = jnp.sqrt(rate[0] * rate[0] + rate[1] * rate[1] + V_FLOOR * V_FLOOR)
        friction = MU_FAST - (MU_FAST - MU_SLOW) * jnp.exp(-RATE_DECAY * speed)
        capacity = friction * t[6:7]
        magnitude = jnp.sqrt(trial[0] * trial[0] + trial[1] * trial[1])
        largest = jnp.maximum(magnitude, capacity)
        largest = jnp.where(real, largest, 1.0)
        force = [jnp.where(stick, trial[c], capacity * trial[c] / largest) for c in range(2)]
        force = [jnp.where(real, f, 0.0) for f in force + [K_VERT * at[2]]]
        stick_k = jnp.where(jnp.logical_and(stick, real), K_STICK, 0.0)
        vert_k = jnp.where(real, K_VERT, 0.0)
        weights = jnp.concatenate([row_hot * v for v in force + [stick_k, vert_k]], axis=0)
        spread = lax.dot_general(
            weights, col_hot, (((1,), (1,)), ((), ())), precision=HIGHEST, preferred_element_type=jnp.float32
        )
        for n in range(5):
            bear[n, 0:CA] = spread[CA * n : CA * (n + 1)]
        tile = jnp.concatenate(force + [jnp.zeros((5, 128), jnp.float32)], axis=0)
        force_in[...] = tile
        for slot in range(1, N_BAND):
            forces[slot] = pltpu.roll(tile, 128 - 4 * slot, 1)
        for slot in range(1, N_BAND):
            force_copy(slot).start()

    @pl.when(jnp.logical_not(low))
    def _():
        bear[:, 0:CA, :] = jnp.zeros((5, CA, NR), jnp.float32)

    bd_first.start()
    bd_last.start()


    for copy in (st_first, st_last):
        copy.wait_recv()
    downward(st_rim_down)
    upward(st_rim_up)

    for copy in (u_first, u_last):
        copy.wait_recv()
    for copy in (p_first, p_last):
        copy.wait_send()
    for copy in (p_first, p_last):
        copy.wait_recv()
    for here, there in ((CA - 1, CA), (0, ROWS - 1)):
        k = face(st[here, lay, :], st[there, lay, :])
        for c in range(3):
            flux = gains[c] * k * (u[c, there, lay, :] - u[c, here, lay, :])
            p[0, c, here, lay, :] = p[0, c, here, lay, :] + flux
            p[0, c, there, lay, :] = p[0, c, there, lay, :] - flux
    downward(p_down)
    upward(p_up)
    for copy in (me_first, me_last):
        copy.wait_recv()
    downward(me_rim_down)
    upward(me_rim_up)

    mean = received(early_b, red_sem.at[2], red_sem.at[3]) * (1.0 / (N_SECTOR * N_BAND * (CA - 2) * LAYERS * NR))
    e128 = jnp.sqrt(jnp.sqrt(jnp.sqrt(mean)))
    scale128 = 2.0 / e128
    scale = jnp.concatenate([scale128, scale128], axis=1)
    from_bands([st_rim_down], [st_rim_up])
    lev = lax.broadcasted_iota(jnp.int32, (LEV, NR), 0)

    @pl.loop(0, ROWS)
    def _(i):
        conductances_of(i, scale)
        k_row[i] = face(st[i], st[lax.rem(i + 1, ROWS)], scale)

    for copy in (bd_first, bd_last):
        copy.wait_recv()

    @pl.when(low)
    def _():
        for c in range(3):
            for i in range(ROWS):
                p[0, c, i, 0:1, :] = p[0, c, i, 0:1, :] - bear[c, i : i + 1, :]

    from_bands([me_down, me_rim_down], [me_up, me_rim_up])

    @pl.loop(0, ROWS)
    def _(i):
        near = k_up[i] + k_dn[i] + k_out[i] + k_in[i] + k_row[i] + k_row[lax.rem(i + ROWS - 1, ROWS)]
        base = scale * me[i] - 2.0
        for h in range(2):
            extra = scale * bear[3 + h, pl.ds(i, 1), :]
            diag[h, i] = base + (h + 1.0) * near + jnp.where(lev == 0, extra, 0.0)

    from_bands([p_down], [p_up])

    sums = {}

    def one_row(j, i, tall=slice(0, LEV)):
        up, dn = lax.rem(i + 1, ROWS), lax.rem(i + ROWS - 1, ROWS)
        kr_up, kr_dn, ku, kd, ko, ki = [
            k[n, tall, :] for k, n in ((k_row, i), (k_row, dn), (k_up, i), (k_dn, i), (k_out, i), (k_in, i))
        ]
        out = []
        for c in range(3):
            whole = p[j, c, i]
            v = whole[tall]
            near = ku * pltpu.roll(whole, LEV - 1, 0)[tall] + kd * pltpu.roll(whole, 1, 0)[tall]
            near = near + ko * pltpu.roll(v, NR - 1, 1) + ki * pltpu.roll(v, 1, 1)
            near = near + kr_up * p[j, c, up, tall, :] + kr_dn * p[j, c, dn, tall, :]
            if c == 2:
                near = near + near
            w = diag[c // 2, i, tall, :] * v - near
            w = 0.5 * w if j == 0 else w - p[j - 1, c, i, tall, :]
            p[j + 1, c, i, tall, :] = w
            out.append(w)
        return out

    for j in range(ITERS):
        pairs = [q for q in PAIRS if q[1] == j + 1 or (j == 0 and q == (0, 0))]

        def own_row(i, acc):
            new = one_row(j, i, lay if j == ITERS - 1 else slice(0, LEV))
            acc = list(acc)
            for c in range(3):
                w = new[c][0:LAYERS]
                for n, (lo, hi) in enumerate(pairs):
                    a = w if lo == j + 1 else p[lo, c, i, lay, :]
                    d = w if hi == j + 1 else p[hi, c, i, lay, :]
                    acc[n] = acc[n] + a * d
            return tuple(acc)

        totals = lax.fori_loop(0, CA, own_row, tuple(jnp.zeros((LAYERS, NR), jnp.float32) for _ in pairs), unroll=2)
        sums.update(zip(pairs, totals))
        wide = ITERS - 1 - j
        if wide:

            @pl.loop(0, 2 * wide, unroll=2)
            def _(i):
                one_row(j, jnp.where(i < wide, CA + i, ROWS - 1 - (i - wide)))

    rows = []
    for q in PAIRS:
        t = jnp.sum(sums[q], axis=0, keepdims=True)
        rows.append(t[:, 0:128] + t[:, 128:256])
    rows = jnp.concatenate(rows + [jnp.zeros((16 - len(PAIRS), 128), jnp.float32)], axis=0)
    eye = lax.broadcasted_iota(jnp.int32, (16, 128), 0) == lax.broadcasted_iota(jnp.int32, (16, 128), 1)
    row = jnp.sum(jnp.where(eye, jnp.sum(rows, axis=1, keepdims=True), 0.0), axis=0, keepdims=True)
    send_row(row, group_a, late_a, red_sem.at[4], red_sem.at[5])
    row = received(late_a, red_sem.at[4], red_sem.at[5])
    send_row(row, group_b, late_b, red_sem.at[6], red_sem.at[7])
    row = received(late_b, red_sem.at[6], red_sem.at[7])
    g = jnp.broadcast_to(jnp.sum(jnp.where(eye, row, 0.0), axis=1, keepdims=True), (16, 128))
    where = {q: n for n, q in enumerate(PAIRS)}
    grams = {q: g[where[q] : where[q] + 1, :] for q in PAIRS}
    xs, rs = coefficients(lambda i, j: grams[(i, j)], e128)
    for n, v in enumerate(xs + rs):
        coef_ref[n : n + 1, :] = v

    @pl.when(jnp.logical_not(low))
    def _():
        force_copy(1).wait_recv()

    force_ref[...] = force_in[...]

    for slot in range(1, N_BAND):

        @pl.when(b == slot)
        def _():
            pack_copy(slot).wait_send()

    @pl.when(low)
    def _():
        for slot in range(1, N_BAND):
            force_copy(slot).wait_send()

    for copy in (st_first, st_last, u_first, u_last, me_first, me_last, bd_first, bd_last):
        copy.wait_send()

    @pl.when(jnp.logical_not(low))
    def _():
        for copy in (u_down, st_down, me_down, st_rim_down, me_rim_down, p_down):
            copy.wait_send()

    @pl.when(jnp.logical_not(high))
    def _():
        for copy in (u_up, st_up, me_up, st_rim_up, me_rim_up, p_up):
            copy.wait_send()


def combine(p, coef, force, inc_hbm, res_hbm, force_hbm, inc, res, out, sems):
    out[...] = force[0:3, 0:4]
    copies = [pltpu.make_async_copy(out, force_hbm, sems.at[0])]
    copies[0].start()
    rows = [jnp.concatenate([coef[n : n + 1, :]] * 2, axis=1) for n in range(2 * ITERS + 1)]
    xs, rs = rows[:ITERS], rows[ITERS:]
    step = CA // 4
    for chunk in range(4):
        span = slice(chunk * step, (chunk + 1) * step)
        for i in range(chunk * step, (chunk + 1) * step):
            for c in range(3):
                vs = [p[j, c, i, 0:LAYERS, :] for j in range(ITERS + 1)]
                a, r = xs[0] * vs[0], rs[0] * vs[0]
                for j in range(1, ITERS):
                    a = a + xs[j] * vs[j]
                for j in range(1, ITERS + 1):
                    r = r + rs[j] * vs[j]
                inc[c, i] = a
                res[c, i] = r
        for n, (src, dst) in enumerate(((inc, inc_hbm), (res, res_hbm))):
            copy = pltpu.make_async_copy(src.at[:, span], dst.at[:, span], sems.at[1 + 2 * chunk + n])
            copy.start()
            copies.append(copy)
    for copy in copies:
        copy.wait()


def per_device(
    given_load,
    displacement,
    mass_coef,
    stiffness,
    bearing_node,
    stick_state,
    slip_prev,
    bearing_old,
    bearing_weight,
):
    f32, i32 = jnp.float32, jnp.int32
    vmem, dma = pltpu.VMEM, pltpu.SemaphoreType.DMA
    field = jax.ShapeDtypeStruct((3, CA, LAYERS, NR), f32)
    in_vmem = pl.BlockSpec(memory_space=vmem)
    in_hbm = pl.BlockSpec(memory_space=pltpu.HBM)
    basis, coef, force = pl.pallas_call(
        kernel,
        out_shape=(
            jax.ShapeDtypeStruct((ITERS + 1, 3, ROWS, LEV, NR), f32),
            jax.ShapeDtypeStruct((16, 128), f32),
            jax.ShapeDtypeStruct((8, 128), f32),
        ),
        in_specs=[in_hbm] * 9,
        out_specs=(in_vmem, in_vmem, in_vmem),
        scratch_shapes=[
            vmem((ROWS, LEV, NR), f32),
            vmem((ROWS, LEV, NR), f32),
            vmem((3, ROWS, LEV, NR), f32),
            vmem((ROWS, LEV, NR), f32),
            vmem((ROWS, LEV, NR), f32),
            vmem((ROWS, LEV, NR), f32),
            vmem((ROWS, LEV, NR), f32),
            vmem((ROWS, LEV, NR), f32),
            vmem((2, ROWS, LEV, NR), f32),
            vmem((5, ROWS, NR), f32),
            vmem((1, 4), i32),
            vmem((1, 4), i32),
            vmem((2, 4), f32),
            vmem((2, 4), f32),
            vmem((1, 4), f32),
            vmem((8, 128), f32),
            vmem((N_BAND, 8, 128), f32),
            vmem((N_BAND, 8, 128), f32),
            vmem((8, 128), f32),
            vmem((8, 1, 128), f32),
            vmem((32, 1, 128), f32),
            vmem((8, 1, 128), f32),
            vmem((32, 1, 128), f32),
            dma((9,)),
            dma((22,)),
            dma((22,)),
            dma((N_BAND,)),
            dma((N_BAND,)),
            dma((N_BAND,)),
            dma((1,)),
            dma((8,)),
        ],
        compiler_params=pltpu.CompilerParams(
            collective_id=0, has_side_effects=True, vmem_limit_bytes=32 * 1024 * 1024
        ),
        name="newton_step",
    )(
        *[
            pltpu.with_memory_space_constraint(a, pltpu.HBM)
            for a in (
                given_load,
                displacement,
                mass_coef,
                stiffness,
                bearing_node.reshape(1, 4),
                stick_state.reshape(1, 4),
                slip_prev,
                bearing_old,
                bearing_weight.reshape(1, 4),
            )
        ]
    )
    return pl.pallas_call(
        combine,
        out_shape=(field, field, jax.ShapeDtypeStruct((3, 4), f32)),
        in_specs=[in_vmem] * 3,
        out_specs=(in_hbm, in_hbm, in_hbm),
        scratch_shapes=[
            vmem((3, CA, LAYERS, NR), f32),
            vmem((3, CA, LAYERS, NR), f32),
            vmem((3, 4), f32),
            dma((9,)),
        ],
        compiler_params=pltpu.CompilerParams(vmem_limit_bytes=16 * 1024 * 1024),
        name="combine",
    )(basis, coef, force)


def solution(mesh):
    return jax.shard_map(
        per_device,
        mesh=mesh,
        in_specs=(
            P(None, "sector", "band", None),
            P(None, "sector", "band", None),
            P("sector", "band", None),
            P("sector", "band", None),
            P(("sector", "band")),
            P(("sector", "band")),
            P(None, ("sector", "band")),
            P(None, ("sector", "band")),
            P(("sector", "band")),
        ),
        out_specs=(
            P(None, "sector", "band", None),
            P(None, "sector", "band", None),
            P(None, ("sector", "band")),
        ),
        check_vma=False,
    )
```

```python
import functools

import jax
import jax.numpy as jnp
from jax import lax
from jax.experimental import pallas as pl
from jax.experimental.pallas import tpu as pltpu
from jax.sharding import PartitionSpec as P

ITERS = 4
K_STICK = 4.0
K_VERT = 8.0
MU_FAST = 0.15
MU_SLOW = 0.04
RATE_GAIN = 2.0
RATE_DECAY = 2.0
V_FLOOR = 0.05
HIGHEST = lax.Precision.HIGHEST
MESH = pl.DeviceIdType.MESH

CA = 8
LAYERS = 16
NR = 256
DEPTH = 4
ROWS = CA + 2 * DEPTH
LEV = LAYERS + 2 * DEPTH
N_SECTOR = 64
N_BAND = 4
NX = 4
NZ = 8
PAIRS = [(0, 0), (0, 1), (1, 1), (0, 2), (1, 2), (2, 2), (0, 3), (1, 3), (2, 3), (3, 3), (0, 4), (1, 4), (2, 4), (3, 4)]


def coefficients(gram, e):
    def apply(d):
        q = [None] * 5

        def add(k, v):
            q[k] = v if q[k] is None else q[k] + v

        for j, dj in enumerate(d):
            t = e * dj
            add(j, t)
            if j == 0:
                add(1, t)
            else:
                add(j + 1, 0.5 * t)
                add(j - 1, 0.5 * t)
        return [v for v in q if v is not None]

    def inner(a, b):
        total = None
        for i, ai in enumerate(a):
            for j, bj in enumerate(b):
                term = ai * bj * gram(min(i, j), max(i, j))
                total = term if total is None else total + term
        return total

    def padded_add(a, b, scale):
        out = []
        for i in range(max(len(a), len(b))):
            if i >= len(a):
                out.append(scale * b[i])
            elif i >= len(b):
                out.append(a[i])
            else:
                out.append(a[i] + scale * b[i])
        return out

    one = jnp.ones_like(gram(0, 0))
    r, d, x = [one], [one], []
    rr = gram(0, 0)
    for k in range(ITERS):
        q = apply(d)
        alpha = rr / inner(d, q)
        x = padded_add(x, d, alpha)
        r = padded_add(r, q, -alpha)
        if k < ITERS - 1:
            new = inner(r, r)
            d = padded_add(r, d, new / rr)
            rr = new
    return x, r


def kernel(
    load_hbm,
    disp_hbm,
    mass_hbm,
    stiff_hbm,
    node_ref,
    stick_ref,
    slip_ref,
    old_ref,
    weight_ref,
    p,
    coef_ref,
    force_ref,
    st,
    me,
    u,
    k_row,
    k_up,
    k_dn,
    k_in,
    k_out,
    diag,
    bear,
    nodes,
    sticks,
    slips,
    olds,
    weighs,
    pack,
    packs,
    forces,
    force_in,
    early_a,
    early_b,
    late_a,
    late_b,
    load_sem,
    send_sem,
    recv_sem,
    pack_send,
    pack_recv,
    force_send,
    force_recv,
    red_sem,
):
    s = lax.axis_index("sector")
    b = lax.axis_index("band")
    z, x, yh = s // 8, lax.rem(s // 2, 4), lax.rem(s, 2)
    s_dn, s_up = lax.rem(s + N_SECTOR - 1, N_SECTOR), lax.rem(s + 1, N_SECTOR)
    low, high = b == 0, b == N_BAND - 1

    def group_a(n):
        k = n + 1
        return ((s // 2) * 2 + lax.rem(yh + k // N_BAND, 2), lax.rem(b + lax.rem(k, N_BAND), N_BAND))

    def group_b(n):
        k = n + 1
        return ((lax.rem(z + k // NX, NZ) * NX + lax.rem(x + lax.rem(k, NX), NX)) * 2 + yh, b)

    size_a, size_b = 2 * N_BAND - 1, NZ * NX - 1

    barrier = pltpu.get_barrier_semaphore()
    for target in ((s_dn, b), (s_up, b)):
        pl.semaphore_signal(barrier, inc=1, device_id=target, device_id_type=MESH)
    for group, size in ((group_a, size_a), (group_b, size_b)):

        @pl.loop(0, size)
        def _(n):
            pl.semaphore_signal(barrier, inc=1, device_id=group(n), device_id_type=MESH)

    local = [
        pltpu.make_async_copy(stiff_hbm, st.at[0:CA, 0:LAYERS, :], load_sem.at[0]),
        pltpu.make_async_copy(disp_hbm, u.at[:, 0:CA, 0:LAYERS, :], load_sem.at[1]),
        pltpu.make_async_copy(mass_hbm, me.at[0:CA, 0:LAYERS, :], load_sem.at[2]),
        pltpu.make_async_copy(load_hbm, p.at[0, :, 0:CA, 0:LAYERS, :], load_sem.at[3]),
    ]
    small = [
        pltpu.make_async_copy(src, dst, load_sem.at[4 + n])
        for n, (src, dst) in enumerate(
            ((node_ref, nodes), (stick_ref, sticks), (slip_ref, slips), (old_ref, olds), (weight_ref, weighs))
        )
    ]
    for copy in local + small:
        copy.start()

    def remote(i, src, dst, target):
        return pltpu.make_async_remote_copy(
            src_ref=src,
            dst_ref=dst,
            send_sem=send_sem.at[i],
            recv_sem=recv_sem.at[i],
            device_id=target,
            device_id_type=MESH,
        )

    own, rim = slice(0, CA), slice(CA, ROWS)
    first, last = slice(0, DEPTH), slice(CA - DEPTH, CA)
    after, before = slice(CA, CA + DEPTH), slice(CA + DEPTH, ROWS)
    lay = slice(0, LAYERS)
    bottom, top = slice(0, DEPTH), slice(LAYERS - DEPTH, LAYERS)
    above, below = slice(LAYERS, LAYERS + DEPTH), slice(LAYERS + DEPTH, LEV)

    b_dn, b_up = (s, lax.rem(b + N_BAND - 1, N_BAND)), (s, lax.rem(b + 1, N_BAND))
    t_dn, t_up = (s_dn, b), (s_up, b)

    u_down = remote(8, disp_hbm.at[:, :, 0:1, :], u.at[:, own, LAYERS : LAYERS + 1, :], b_dn)
    u_up = remote(9, disp_hbm.at[:, :, LAYERS - 1 : LAYERS, :], u.at[:, own, LEV - 1 : LEV, :], b_up)
    st_down = remote(6, stiff_hbm.at[:, bottom, :], st.at[own, above, :], b_dn)
    st_up = remote(7, stiff_hbm.at[:, top, :], st.at[own, below, :], b_up)
    me_down = remote(10, mass_hbm.at[:, bottom, :], me.at[own, above, :], b_dn)
    me_up = remote(11, mass_hbm.at[:, top, :], me.at[own, below, :], b_up)
    st_first = remote(0, stiff_hbm.at[first], st.at[after, lay, :], t_dn)
    st_last = remote(1, stiff_hbm.at[last], st.at[before, lay, :], t_up)
    me_first = remote(2, mass_hbm.at[0 : DEPTH - 1], me.at[CA : CA + DEPTH - 1, lay, :], t_dn)
    me_last = remote(3, mass_hbm.at[CA - DEPTH + 1 : CA], me.at[CA + DEPTH + 1 : ROWS, lay, :], t_up)
    u_first = remote(4, disp_hbm.at[:, 0:1], u.at[:, CA : CA + 1, lay, :], t_dn)
    u_last = remote(5, disp_hbm.at[:, CA - 1 : CA], u.at[:, ROWS - 1 : ROWS, lay, :], t_up)
    st_rim_down = remote(12, st.at[rim, bottom, :], st.at[rim, above, :], b_dn)
    st_rim_up = remote(13, st.at[rim, top, :], st.at[rim, below, :], b_up)
    me_rim_down = remote(14, me.at[rim, bottom, :], me.at[rim, above, :], b_dn)
    me_rim_up = remote(15, me.at[rim, top, :], me.at[rim, below, :], b_up)
    bd_first = remote(16, bear.at[:, first, :], bear.at[:, after, :], t_dn)
    bd_last = remote(17, bear.at[:, last, :], bear.at[:, before, :], t_up)
    p_first = remote(18, p.at[0, :, first, lay, :], p.at[0, :, after, lay, :], t_dn)
    p_last = remote(19, p.at[0, :, last, lay, :], p.at[0, :, before, lay, :], t_up)
    less = DEPTH - 1
    p_down = [
        remote(20, p.at[0, :, own, bottom, :], p.at[0, :, own, above, :], b_dn),
        remote(22, p.at[0, :, CA : CA + less, 0:less, :], p.at[0, :, CA : CA + less, LAYERS : LAYERS + less, :], b_dn),
        remote(23, p.at[0, :, ROWS - less : ROWS, 0:less, :], p.at[0, :, ROWS - less : ROWS, LAYERS : LAYERS + less, :], b_dn),
    ]
    far, low_far = slice(LAYERS - less, LAYERS), slice(LEV - less, LEV)
    p_up = [
        remote(21, p.at[0, :, own, top, :], p.at[0, :, own, below, :], b_up),
        remote(24, p.at[0, :, CA : CA + less, far, :], p.at[0, :, CA : CA + less, low_far, :], b_up),
        remote(25, p.at[0, :, ROWS - less : ROWS, far, :], p.at[0, :, ROWS - less : ROWS, low_far, :], b_up),
    ]

    def pack_copy(slot):
        return pltpu.make_async_remote_copy(
            src_ref=pack,
            dst_ref=packs.at[slot],
            send_sem=pack_send.at[slot],
            recv_sem=pack_recv.at[slot],
            device_id=(s, 0),
            device_id_type=MESH,
        )

    def force_copy(slot):
        return pltpu.make_async_remote_copy(
            src_ref=forces.at[slot],
            dst_ref=force_in,
            send_sem=force_send.at[slot],
            recv_sem=force_recv.at[0],
            device_id=(s, slot),
            device_id_type=MESH,
        )

    def downward(*copies):
        @pl.when(jnp.logical_not(low))
        def _():
            for copy in copies:
                copy.start()

    def upward(*copies):
        @pl.when(jnp.logical_not(high))
        def _():
            for copy in copies:
                copy.start()

    def from_bands(downs, ups):
        @pl.when(jnp.logical_not(high))
        def _():
            for copy in downs:
                copy.wait_recv()

        @pl.when(jnp.logical_not(low))
        def _():
            for copy in ups:
                copy.wait_recv()

    @pl.when(low)
    def _():
        st[:, LEV - DEPTH : LEV, :] = jnp.zeros((ROWS, DEPTH, NR), jnp.float32)
        me[:, LEV - DEPTH : LEV, :] = jnp.zeros((ROWS, DEPTH, NR), jnp.float32)
        u[:, 0:CA, LEV - 1 : LEV, :] = jnp.zeros((3, CA, 1, NR), jnp.float32)
        p[0, :, :, LEV - DEPTH : LEV, :] = jnp.zeros((3, ROWS, DEPTH, NR), jnp.float32)

    @pl.when(high)
    def _():
        st[:, LAYERS : LAYERS + DEPTH, :] = jnp.zeros((ROWS, DEPTH, NR), jnp.float32)
        me[:, LAYERS : LAYERS + DEPTH, :] = jnp.zeros((ROWS, DEPTH, NR), jnp.float32)
        u[:, 0:CA, LAYERS : LAYERS + 1, :] = jnp.zeros((3, CA, 1, NR), jnp.float32)
        p[0, :, :, LAYERS : LAYERS + DEPTH, :] = jnp.zeros((3, ROWS, DEPTH, NR), jnp.float32)

    def face(a, c, scale=1.0):
        return (2.0 * scale) * a * c / jnp.maximum(a + c, 0.25)

    def send_row(row, group, slots, send, recv):
        n_others = slots.shape[0] - 1
        slots[n_others] = row

        @pl.loop(0, n_others)
        def _(n):
            pltpu.make_async_remote_copy(
                src_ref=slots.at[n_others],
                dst_ref=slots.at[n],
                send_sem=send,
                recv_sem=recv,
                device_id=group(n),
                device_id_type=MESH,
            ).start()

    def received(slots, send, recv):
        others = slots.at[0 : slots.shape[0] - 1]
        pltpu.make_async_copy(others, others, recv).wait()
        pltpu.make_async_copy(others, others, send).wait()
        return jnp.sum(slots[...], axis=0)

    local[0].wait()
    local[2].wait()
    k_row[0, lay, :] = face(st[0, lay, :], st[1, lay, :])

    def powers_of(i, total):
        k = face(st[i, lay, :], st[i + 1, lay, :])
        d = me[i, lay, :] + 6.0 * (k + k_row[i - 1, lay, :])
        k_row[i, lay, :] = k
        d = d * d
        d = d * d
        return total + d * d

    powers = lax.fori_loop(1, CA - 1, powers_of, jnp.zeros((LAYERS, NR), jnp.float32), unroll=True)
    total = jnp.sum(jnp.sum(powers, axis=0, keepdims=True), axis=1, keepdims=True)
    pl.semaphore_wait(barrier, 2 + size_a + size_b)

    send_row(jnp.broadcast_to(total, (1, 128)), group_a, early_a, red_sem.at[0], red_sem.at[1])
    downward(u_down, st_down)
    upward(u_up, st_up)
    for copy in (u_first, u_last):
        copy.start()
    for copy in (st_first, st_last):
        copy.start()
    downward(me_down)
    upward(me_up)
    pack[...] = jnp.zeros_like(pack)
    me[CA + DEPTH - 1 : CA + DEPTH + 1, lay, :] = jnp.zeros((2, LAYERS, NR), jnp.float32)
    for copy in small:
        copy.wait()
    pack[0:1, 0:4] = nodes[...].astype(jnp.float32)
    pack[1:2, 0:4] = sticks[...].astype(jnp.float32)
    pack[2:4, 0:4] = slips[...]
    pack[4:6, 0:4] = olds[...]
    pack[6:7, 0:4] = weighs[...]

    for slot in range(1, N_BAND):

        @pl.when(b == slot)
        def _():
            pack_copy(slot).start()


    lane = lax.broadcasted_iota(jnp.int32, (LEV, NR), 1)

    def conductances_of(i, scale=1.0):
        a = st[i]
        ku = face(a, pltpu.roll(a, LEV - 1, 0), scale)
        ko = jnp.where(lane == NR - 1, 0.0, face(a, pltpu.roll(a, NR - 1, 1), scale))
        k_up[i] = ku
        k_dn[i] = pltpu.roll(ku, 1, 0)
        k_out[i] = ko
        k_in[i] = pltpu.roll(ko, 1, 1)

    from_bands([u_down, st_down], [u_up, st_up])

    @pl.loop(0, CA)
    def _(i):
        conductances_of(i)

    local[1].wait()
    local[3].wait()

    gains = (1.0, 1.0, 2.0)

    @pl.loop(0, CA)
    def _(i):
        up, dn = jnp.minimum(i + 1, CA - 1), jnp.maximum(i - 1, 0)
        kr_up = k_row[jnp.minimum(i, CA - 2), lay, :]
        kr_dn = k_row[dn, lay, :]
        ku, kd, ko, ki = k_up[i, lay, :], k_dn[i, lay, :], k_out[i, lay, :], k_in[i, lay, :]
        m = me[i, lay, :]
        for c in range(3):
            whole = u[c, i]
            v = whole[0:LAYERS]
            above_v = pltpu.roll(whole, LEV - 1, 0)[0:LAYERS]
            below_v = pltpu.roll(whole, 1, 0)[0:LAYERS]
            acc = ku * (above_v - v) + kd * (below_v - v)
            acc = acc + ko * (pltpu.roll(v, NR - 1, 1) - v) + ki * (pltpu.roll(v, 1, 1) - v)
            acc = acc + kr_up * (u[c, up, lay, :] - v) + kr_dn * (u[c, dn, lay, :] - v)
            p[0, c, i, lay, :] = p[0, c, i, lay, :] - m * v + gains[c] * acc
    for copy in (p_first, p_last, me_first, me_last):
        copy.start()
    send_row(received(early_a, red_sem.at[0], red_sem.at[1]), group_b, early_b, red_sem.at[2], red_sem.at[3])

    @pl.when(low)
    def _():
        packs[0] = pack[...]
        for slot in range(1, N_BAND):
            pack_copy(slot).wait_recv()
        t = packs[0]
        for slot in range(1, N_BAND):
            t = t + pltpu.roll(packs[slot], 4 * slot, 1)
        t = t[:, 0:128]
        node = t[0:1, :].astype(jnp.int32)
        stick = t[1:2, :] > 0.5
        row_of = node // NR
        col_of = lax.rem(node, NR)
        real = lax.broadcasted_iota(jnp.int32, (1, 128), 1) < 4 * N_BAND
        col_hot = jnp.where(
            jnp.logical_and(lax.broadcasted_iota(jnp.int32, (NR, 128), 0) == col_of, real), 1.0, 0.0
        ).astype(jnp.float32)
        row_hot = jnp.where(lax.broadcasted_iota(jnp.int32, (CA, 128), 0) == row_of, 1.0, 0.0).astype(jnp.float32)
        raft = jnp.concatenate([u[c, r, 0:1, :] for c in range(3) for r in range(CA)], axis=0)
        picked = jnp.dot(raft, col_hot, precision=HIGHEST, preferred_element_type=jnp.float32)
        at = [jnp.sum(picked[CA * c : CA * (c + 1)] * row_hot, axis=0, keepdims=True) for c in range(3)]
        trial = [K_STICK * (at[c] - t[2 + c : 3 + c]) for c in range(2)]
        rate = [RATE_GAIN * (at[c] - t[4 + c : 5 + c]) for c in range(2)]
        speed = jnp.sqrt(rate[0] * rate[0] + rate[1] * rate[1] + V_FLOOR * V_FLOOR)
        friction = MU_FAST - (MU_FAST - MU_SLOW) * jnp.exp(-RATE_DECAY * speed)
        capacity = friction * t[6:7]
        magnitude = jnp.sqrt(trial[0] * trial[0] + trial[1] * trial[1])
        largest = jnp.maximum(magnitude, capacity)
        largest = jnp.where(real, largest, 1.0)
        force = [jnp.where(stick, trial[c], capacity * trial[c] / largest) for c in range(2)]
        force = [jnp.where(real, f, 0.0) for f in force + [K_VERT * at[2]]]
        stick_k = jnp.where(jnp.logical_and(stick, real), K_STICK, 0.0)
        vert_k = jnp.where(real, K_VERT, 0.0)
        weights = jnp.concatenate([row_hot * v for v in force + [stick_k, vert_k]], axis=0)
        spread = lax.dot_general(
            weights, col_hot, (((1,), (1,)), ((), ())), precision=HIGHEST, preferred_element_type=jnp.float32
        )
        for n in range(5):
            bear[n, 0:CA] = spread[CA * n : CA * (n + 1)]
        tile = jnp.concatenate(force + [jnp.zeros((5, 128), jnp.float32)], axis=0)
        force_in[...] = tile
        for slot in range(1, N_BAND):
            forces[slot] = pltpu.roll(tile, 128 - 4 * slot, 1)
        for slot in range(1, N_BAND):
            force_copy(slot).start()

    @pl.when(jnp.logical_not(low))
    def _():
        bear[:, 0:CA, :] = jnp.zeros((5, CA, NR), jnp.float32)

    bd_first.start()
    bd_last.start()


    for copy in (st_first, st_last):
        copy.wait_recv()
    downward(st_rim_down)
    upward(st_rim_up)

    for copy in (u_first, u_last):
        copy.wait_recv()
    for copy in (p_first, p_last):
        copy.wait_send()
    for copy in (p_first, p_last):
        copy.wait_recv()
    for here, there in ((CA - 1, CA), (0, ROWS - 1)):
        k = face(st[here, lay, :], st[there, lay, :])
        for c in range(3):
            flux = gains[c] * k * (u[c, there, lay, :] - u[c, here, lay, :])
            p[0, c, here, lay, :] = p[0, c, here, lay, :] + flux
            p[0, c, there, lay, :] = p[0, c, there, lay, :] - flux
    downward(*p_down)
    upward(*p_up)
    for copy in (me_first, me_last):
        copy.wait_recv()
    downward(me_rim_down)
    upward(me_rim_up)

    mean = received(early_b, red_sem.at[2], red_sem.at[3]) * (1.0 / (N_SECTOR * N_BAND * (CA - 2) * LAYERS * NR))
    e128 = jnp.sqrt(jnp.sqrt(jnp.sqrt(mean)))
    scale128 = 2.0 / e128
    scale = jnp.concatenate([scale128, scale128], axis=1)
    from_bands([st_rim_down], [st_rim_up])
    lev = lax.broadcasted_iota(jnp.int32, (LEV, NR), 0)

    @pl.loop(0, ROWS)
    def _(i):
        conductances_of(i, scale)
        k_row[i] = face(st[i], st[lax.rem(i + 1, ROWS)], scale)

    for copy in (bd_first, bd_last):
        copy.wait_recv()

    @pl.when(low)
    def _():
        for c in range(3):
            for i in range(ROWS):
                p[0, c, i, 0:1, :] = p[0, c, i, 0:1, :] - bear[c, i : i + 1, :]

    from_bands([me_down, me_rim_down], [me_up, me_rim_up])

    @pl.loop(0, ROWS)
    def _(i):
        near = k_up[i] + k_dn[i] + k_out[i] + k_in[i] + k_row[i] + k_row[lax.rem(i + ROWS - 1, ROWS)]
        base = scale * me[i] - 2.0
        for h in range(2):
            extra = scale * bear[3 + h, pl.ds(i, 1), :]
            diag[h, i] = base + (h + 1.0) * near + jnp.where(lev == 0, extra, 0.0)

    from_bands(p_down, p_up)

    sums = {}

    def one_row(j, i, tall=slice(0, LEV)):
        up, dn = lax.rem(i + 1, ROWS), lax.rem(i + ROWS - 1, ROWS)
        kr_up, kr_dn, ku, kd, ko, ki = [
            k[n, tall, :] for k, n in ((k_row, i), (k_row, dn), (k_up, i), (k_dn, i), (k_out, i), (k_in, i))
        ]
        out = []
        for c in range(3):
            whole = p[j, c, i]
            v = whole[tall]
            near = ku * pltpu.roll(whole, LEV - 1, 0)[tall] + kd * pltpu.roll(whole, 1, 0)[tall]
            near = near + ko * pltpu.roll(v, NR - 1, 1) + ki * pltpu.roll(v, 1, 1)
            near = near + kr_up * p[j, c, up, tall, :] + kr_dn * p[j, c, dn, tall, :]
            if c == 2:
                near = near + near
            w = diag[c // 2, i, tall, :] * v - near
            w = 0.5 * w if j == 0 else w - p[j - 1, c, i, tall, :]
            p[j + 1, c, i, tall, :] = w
            out.append(w)
        return out

    for j in range(ITERS):
        pairs = [q for q in PAIRS if q[1] == j + 1 or (j == 0 and q == (0, 0))]

        def own_row(i, acc):
            new = one_row(j, i, lay if j == ITERS - 1 else slice(0, LEV))
            acc = list(acc)
            for c in range(3):
                w = new[c][0:LAYERS]
                for n, (lo, hi) in enumerate(pairs):
                    a = w if lo == j + 1 else p[lo, c, i, lay, :]
                    d = w if hi == j + 1 else p[hi, c, i, lay, :]
                    acc[n] = acc[n] + a * d
            return tuple(acc)

        totals = lax.fori_loop(0, CA, own_row, tuple(jnp.zeros((LAYERS, NR), jnp.float32) for _ in pairs), unroll=2)
        sums.update(zip(pairs, totals))
        wide = ITERS - 1 - j
        if wide:

            @pl.loop(0, 2 * wide, unroll=2)
            def _(i):
                one_row(j, jnp.where(i < wide, CA + i, ROWS - 1 - (i - wide)))

    rows = []
    for q in PAIRS:
        t = jnp.sum(sums[q], axis=0, keepdims=True)
        rows.append(t[:, 0:128] + t[:, 128:256])
    rows = jnp.concatenate(rows + [jnp.zeros((16 - len(PAIRS), 128), jnp.float32)], axis=0)
    eye = lax.broadcasted_iota(jnp.int32, (16, 128), 0) == lax.broadcasted_iota(jnp.int32, (16, 128), 1)
    row = jnp.sum(jnp.where(eye, jnp.sum(rows, axis=1, keepdims=True), 0.0), axis=0, keepdims=True)
    send_row(row, group_a, late_a, red_sem.at[4], red_sem.at[5])
    row = received(late_a, red_sem.at[4], red_sem.at[5])
    send_row(row, group_b, late_b, red_sem.at[6], red_sem.at[7])
    row = received(late_b, red_sem.at[6], red_sem.at[7])
    g = jnp.broadcast_to(jnp.sum(jnp.where(eye, row, 0.0), axis=1, keepdims=True), (16, 128))
    where = {q: n for n, q in enumerate(PAIRS)}
    grams = {q: g[where[q] : where[q] + 1, :] for q in PAIRS}
    xs, rs = coefficients(lambda i, j: grams[(i, j)], e128)
    for n, v in enumerate(xs + rs):
        coef_ref[n : n + 1, :] = v

    @pl.when(jnp.logical_not(low))
    def _():
        force_copy(1).wait_recv()

    force_ref[...] = force_in[...]

    for slot in range(1, N_BAND):

        @pl.when(b == slot)
        def _():
            pack_copy(slot).wait_send()

    @pl.when(low)
    def _():
        for slot in range(1, N_BAND):
            force_copy(slot).wait_send()

    for copy in (st_first, st_last, u_first, u_last, me_first, me_last, bd_first, bd_last):
        copy.wait_send()

    @pl.when(jnp.logical_not(low))
    def _():
        for copy in [u_down, st_down, me_down, st_rim_down, me_rim_down] + p_down:
            copy.wait_send()

    @pl.when(jnp.logical_not(high))
    def _():
        for copy in [u_up, st_up, me_up, st_rim_up, me_rim_up] + p_up:
            copy.wait_send()


def combine(p, coef, force, inc_hbm, res_hbm, force_hbm, inc, res, out, sems):
    out[...] = force[0:3, 0:4]
    copies = [pltpu.make_async_copy(out, force_hbm, sems.at[0])]
    copies[0].start()
    rows = [jnp.concatenate([coef[n : n + 1, :]] * 2, axis=1) for n in range(2 * ITERS + 1)]
    xs, rs = rows[:ITERS], rows[ITERS:]
    step = CA // 4
    for chunk in range(4):
        span = slice(chunk * step, (chunk + 1) * step)
        for i in range(chunk * step, (chunk + 1) * step):
            for c in range(3):
                vs = [p[j, c, i, 0:LAYERS, :] for j in range(ITERS + 1)]
                a, r = xs[0] * vs[0], rs[0] * vs[0]
                for j in range(1, ITERS):
                    a = a + xs[j] * vs[j]
                for j in range(1, ITERS + 1):
                    r = r + rs[j] * vs[j]
                inc[c, i] = a
                res[c, i] = r
        for n, (src, dst) in enumerate(((inc, inc_hbm), (res, res_hbm))):
            copy = pltpu.make_async_copy(src.at[:, span], dst.at[:, span], sems.at[1 + 2 * chunk + n])
            copy.start()
            copies.append(copy)
    for copy in copies:
        copy.wait()


def per_device(
    given_load,
    displacement,
    mass_coef,
    stiffness,
    bearing_node,
    stick_state,
    slip_prev,
    bearing_old,
    bearing_weight,
):
    f32, i32 = jnp.float32, jnp.int32
    vmem, dma = pltpu.VMEM, pltpu.SemaphoreType.DMA
    field = jax.ShapeDtypeStruct((3, CA, LAYERS, NR), f32)
    in_vmem = pl.BlockSpec(memory_space=vmem)
    in_hbm = pl.BlockSpec(memory_space=pltpu.HBM)
    basis, coef, force = pl.pallas_call(
        kernel,
        out_shape=(
            jax.ShapeDtypeStruct((ITERS + 1, 3, ROWS, LEV, NR), f32),
            jax.ShapeDtypeStruct((16, 128), f32),
            jax.ShapeDtypeStruct((8, 128), f32),
        ),
        in_specs=[in_hbm] * 9,
        out_specs=(in_vmem, in_vmem, in_vmem),
        scratch_shapes=[
            vmem((ROWS, LEV, NR), f32),
            vmem((ROWS, LEV, NR), f32),
            vmem((3, ROWS, LEV, NR), f32),
            vmem((ROWS, LEV, NR), f32),
            vmem((ROWS, LEV, NR), f32),
            vmem((ROWS, LEV, NR), f32),
            vmem((ROWS, LEV, NR), f32),
            vmem((ROWS, LEV, NR), f32),
            vmem((2, ROWS, LEV, NR), f32),
            vmem((5, ROWS, NR), f32),
            vmem((1, 4), i32),
            vmem((1, 4), i32),
            vmem((2, 4), f32),
            vmem((2, 4), f32),
            vmem((1, 4), f32),
            vmem((8, 128), f32),
            vmem((N_BAND, 8, 128), f32),
            vmem((N_BAND, 8, 128), f32),
            vmem((8, 128), f32),
            vmem((8, 1, 128), f32),
            vmem((32, 1, 128), f32),
            vmem((8, 1, 128), f32),
            vmem((32, 1, 128), f32),
            dma((9,)),
            dma((26,)),
            dma((26,)),
            dma((N_BAND,)),
            dma((N_BAND,)),
            dma((N_BAND,)),
            dma((1,)),
            dma((8,)),
        ],
        compiler_params=pltpu.CompilerParams(
            collective_id=0, has_side_effects=True, vmem_limit_bytes=32 * 1024 * 1024
        ),
        name="newton_step",
    )(
        *[
            pltpu.with_memory_space_constraint(a, pltpu.HBM)
            for a in (
                given_load,
                displacement,
                mass_coef,
                stiffness,
                bearing_node.reshape(1, 4),
                stick_state.reshape(1, 4),
                slip_prev,
                bearing_old,
                bearing_weight.reshape(1, 4),
            )
        ]
    )
    return pl.pallas_call(
        combine,
        out_shape=(field, field, jax.ShapeDtypeStruct((3, 4), f32)),
        in_specs=[in_vmem] * 3,
        out_specs=(in_hbm, in_hbm, in_hbm),
        scratch_shapes=[
            vmem((3, CA, LAYERS, NR), f32),
            vmem((3, CA, LAYERS, NR), f32),
            vmem((3, 4), f32),
            dma((9,)),
        ],
        compiler_params=pltpu.CompilerParams(vmem_limit_bytes=16 * 1024 * 1024),
        name="combine",
    )(basis, coef, force)


def solution(mesh):
    return jax.shard_map(
        per_device,
        mesh=mesh,
        in_specs=(
            P(None, "sector", "band", None),
            P(None, "sector", "band", None),
            P("sector", "band", None),
            P("sector", "band", None),
            P(("sector", "band")),
            P(("sector", "band")),
            P(None, ("sector", "band")),
            P(None, ("sector", "band")),
            P(("sector", "band")),
        ),
        out_specs=(
            P(None, "sector", "band", None),
            P(None, "sector", "band", None),
            P(None, ("sector", "band")),
        ),
        check_vma=False,
    )
```

```python
import functools

import jax
import jax.numpy as jnp
from jax import lax
from jax.experimental import pallas as pl
from jax.experimental.pallas import tpu as pltpu
from jax.sharding import PartitionSpec as P

ITERS = 4
K_STICK = 4.0
K_VERT = 8.0
MU_FAST = 0.15
MU_SLOW = 0.04
RATE_GAIN = 2.0
RATE_DECAY = 2.0
V_FLOOR = 0.05
HIGHEST = lax.Precision.HIGHEST
MESH = pl.DeviceIdType.MESH

CA = 8
LAYERS = 16
NR = 256
DEPTH = 4
ROWS = CA + 2 * DEPTH
LEV = LAYERS + 2 * DEPTH
N_SECTOR = 64
N_BAND = 4
NX = 4
NZ = 8
PAIRS = [(0, 0), (0, 1), (1, 1), (0, 2), (1, 2), (2, 2), (0, 3), (1, 3), (2, 3), (3, 3), (0, 4), (1, 4), (2, 4), (3, 4)]


def coefficients(gram, e):
    def apply(d):
        q = [None] * 5

        def add(k, v):
            q[k] = v if q[k] is None else q[k] + v

        for j, dj in enumerate(d):
            t = e * dj
            add(j, t)
            if j == 0:
                add(1, t)
            else:
                add(j + 1, 0.5 * t)
                add(j - 1, 0.5 * t)
        return [v for v in q if v is not None]

    def inner(a, b):
        total = None
        for i, ai in enumerate(a):
            for j, bj in enumerate(b):
                term = ai * bj * gram(min(i, j), max(i, j))
                total = term if total is None else total + term
        return total

    def padded_add(a, b, scale):
        out = []
        for i in range(max(len(a), len(b))):
            if i >= len(a):
                out.append(scale * b[i])
            elif i >= len(b):
                out.append(a[i])
            else:
                out.append(a[i] + scale * b[i])
        return out

    one = jnp.ones_like(gram(0, 0))
    r, d, x = [one], [one], []
    rr = gram(0, 0)
    for k in range(ITERS):
        q = apply(d)
        alpha = rr / inner(d, q)
        x = padded_add(x, d, alpha)
        r = padded_add(r, q, -alpha)
        if k < ITERS - 1:
            new = inner(r, r)
            d = padded_add(r, d, new / rr)
            rr = new
    return x, r


def kernel(
    load_hbm,
    disp_hbm,
    mass_hbm,
    stiff_hbm,
    node_ref,
    stick_ref,
    slip_ref,
    old_ref,
    weight_ref,
    p,
    coef_ref,
    force_ref,
    st,
    me,
    u,
    k_row,
    k_up,
    k_dn,
    k_in,
    k_out,
    diag,
    bear,
    nodes,
    sticks,
    slips,
    olds,
    weighs,
    pack,
    packs,
    forces,
    force_in,
    early_a,
    early_b,
    late_a,
    late_b,
    load_sem,
    send_sem,
    recv_sem,
    pack_send,
    pack_recv,
    force_send,
    force_recv,
    red_sem,
):
    s = lax.axis_index("sector")
    b = lax.axis_index("band")
    z, x, yh = s // 8, lax.rem(s // 2, 4), lax.rem(s, 2)
    s_dn, s_up = lax.rem(s + N_SECTOR - 1, N_SECTOR), lax.rem(s + 1, N_SECTOR)
    low, high = b == 0, b == N_BAND - 1

    def group_a(n):
        k = n + 1
        return ((s // 2) * 2 + lax.rem(yh + k // N_BAND, 2), lax.rem(b + lax.rem(k, N_BAND), N_BAND))

    def group_b(n):
        k = n + 1
        return ((lax.rem(z + k // NX, NZ) * NX + lax.rem(x + lax.rem(k, NX), NX)) * 2 + yh, b)

    size_a, size_b = 2 * N_BAND - 1, NZ * NX - 1

    barrier = pltpu.get_barrier_semaphore()
    for target in ((s_dn, b), (s_up, b)):
        pl.semaphore_signal(barrier, inc=1, device_id=target, device_id_type=MESH)
    for group, size in ((group_a, size_a), (group_b, size_b)):

        @pl.loop(0, size)
        def _(n):
            pl.semaphore_signal(barrier, inc=1, device_id=group(n), device_id_type=MESH)

    local = [
        pltpu.make_async_copy(stiff_hbm, st.at[0:CA, 0:LAYERS, :], load_sem.at[0]),
        pltpu.make_async_copy(disp_hbm, u.at[:, 0:CA, 0:LAYERS, :], load_sem.at[1]),
        pltpu.make_async_copy(mass_hbm, me.at[0:CA, 0:LAYERS, :], load_sem.at[2]),
        pltpu.make_async_copy(load_hbm, p.at[0, :, 0:CA, 0:LAYERS, :], load_sem.at[3]),
    ]
    small = [
        pltpu.make_async_copy(src, dst, load_sem.at[4 + n])
        for n, (src, dst) in enumerate(
            ((node_ref, nodes), (stick_ref, sticks), (slip_ref, slips), (old_ref, olds), (weight_ref, weighs))
        )
    ]
    for copy in local + small:
        copy.start()

    def remote(i, src, dst, target):
        return pltpu.make_async_remote_copy(
            src_ref=src,
            dst_ref=dst,
            send_sem=send_sem.at[i],
            recv_sem=recv_sem.at[i],
            device_id=target,
            device_id_type=MESH,
        )

    own, rim = slice(0, CA), slice(CA, ROWS)
    first, last = slice(0, DEPTH), slice(CA - DEPTH, CA)
    after, before = slice(CA, CA + DEPTH), slice(CA + DEPTH, ROWS)
    lay = slice(0, LAYERS)
    bottom, top = slice(0, DEPTH), slice(LAYERS - DEPTH, LAYERS)
    above, below = slice(LAYERS, LAYERS + DEPTH), slice(LAYERS + DEPTH, LEV)

    b_dn, b_up = (s, lax.rem(b + N_BAND - 1, N_BAND)), (s, lax.rem(b + 1, N_BAND))
    t_dn, t_up = (s_dn, b), (s_up, b)

    u_down = remote(8, disp_hbm.at[:, :, 0:1, :], u.at[:, own, LAYERS : LAYERS + 1, :], b_dn)
    u_up = remote(9, disp_hbm.at[:, :, LAYERS - 1 : LAYERS, :], u.at[:, own, LEV - 1 : LEV, :], b_up)
    st_down = remote(6, stiff_hbm.at[:, bottom, :], st.at[own, above, :], b_dn)
    st_up = remote(7, stiff_hbm.at[:, top, :], st.at[own, below, :], b_up)
    me_down = remote(10, mass_hbm.at[:, bottom, :], me.at[own, above, :], b_dn)
    me_up = remote(11, mass_hbm.at[:, top, :], me.at[own, below, :], b_up)
    st_first = remote(0, stiff_hbm.at[first], st.at[after, lay, :], t_dn)
    st_last = remote(1, stiff_hbm.at[last], st.at[before, lay, :], t_up)
    me_first = remote(2, mass_hbm.at[0 : DEPTH - 1], me.at[CA : CA + DEPTH - 1, lay, :], t_dn)
    me_last = remote(3, mass_hbm.at[CA - DEPTH + 1 : CA], me.at[CA + DEPTH + 1 : ROWS, lay, :], t_up)
    u_first = remote(4, disp_hbm.at[:, 0:1], u.at[:, CA : CA + 1, lay, :], t_dn)
    u_last = remote(5, disp_hbm.at[:, CA - 1 : CA], u.at[:, ROWS - 1 : ROWS, lay, :], t_up)
    st_rim_down = remote(12, st.at[rim, bottom, :], st.at[rim, above, :], b_dn)
    st_rim_up = remote(13, st.at[rim, top, :], st.at[rim, below, :], b_up)
    me_rim_down = remote(14, me.at[rim, bottom, :], me.at[rim, above, :], b_dn)
    me_rim_up = remote(15, me.at[rim, top, :], me.at[rim, below, :], b_up)
    bd_first = remote(16, bear.at[:, first, :], bear.at[:, after, :], t_dn)
    bd_last = remote(17, bear.at[:, last, :], bear.at[:, before, :], t_up)
    p_first = remote(18, p.at[0, :, first, lay, :], p.at[0, :, after, lay, :], t_dn)
    p_last = remote(19, p.at[0, :, last, lay, :], p.at[0, :, before, lay, :], t_up)
    less = DEPTH - 1
    p_down = [
        remote(20, p.at[0, :, own, bottom, :], p.at[0, :, own, above, :], b_dn),
        remote(22, p.at[0, :, CA : CA + less, 0:less, :], p.at[0, :, CA : CA + less, LAYERS : LAYERS + less, :], b_dn),
        remote(23, p.at[0, :, ROWS - less : ROWS, 0:less, :], p.at[0, :, ROWS - less : ROWS, LAYERS : LAYERS + less, :], b_dn),
    ]
    far, low_far = slice(LAYERS - less, LAYERS), slice(LEV - less, LEV)
    p_up = [
        remote(21, p.at[0, :, own, top, :], p.at[0, :, own, below, :], b_up),
        remote(24, p.at[0, :, CA : CA + less, far, :], p.at[0, :, CA : CA + less, low_far, :], b_up),
        remote(25, p.at[0, :, ROWS - less : ROWS, far, :], p.at[0, :, ROWS - less : ROWS, low_far, :], b_up),
    ]

    def pack_copy(slot):
        return pltpu.make_async_remote_copy(
            src_ref=pack,
            dst_ref=packs.at[slot],
            send_sem=pack_send.at[slot],
            recv_sem=pack_recv.at[slot],
            device_id=(s, 0),
            device_id_type=MESH,
        )

    def force_copy(slot):
        return pltpu.make_async_remote_copy(
            src_ref=forces.at[slot],
            dst_ref=force_in,
            send_sem=force_send.at[slot],
            recv_sem=force_recv.at[0],
            device_id=(s, slot),
            device_id_type=MESH,
        )

    def downward(*copies):
        @pl.when(jnp.logical_not(low))
        def _():
            for copy in copies:
                copy.start()

    def upward(*copies):
        @pl.when(jnp.logical_not(high))
        def _():
            for copy in copies:
                copy.start()

    def from_bands(downs, ups):
        @pl.when(jnp.logical_not(high))
        def _():
            for copy in downs:
                copy.wait_recv()

        @pl.when(jnp.logical_not(low))
        def _():
            for copy in ups:
                copy.wait_recv()

    @pl.when(low)
    def _():
        st[:, LEV - DEPTH : LEV, :] = jnp.zeros((ROWS, DEPTH, NR), jnp.float32)
        me[:, LEV - DEPTH : LEV, :] = jnp.zeros((ROWS, DEPTH, NR), jnp.float32)
        u[:, 0:CA, LEV - 1 : LEV, :] = jnp.zeros((3, CA, 1, NR), jnp.float32)
        p[0, :, :, LEV - DEPTH : LEV, :] = jnp.zeros((3, ROWS, DEPTH, NR), jnp.float32)

    @pl.when(high)
    def _():
        st[:, LAYERS : LAYERS + DEPTH, :] = jnp.zeros((ROWS, DEPTH, NR), jnp.float32)
        me[:, LAYERS : LAYERS + DEPTH, :] = jnp.zeros((ROWS, DEPTH, NR), jnp.float32)
        u[:, 0:CA, LAYERS : LAYERS + 1, :] = jnp.zeros((3, CA, 1, NR), jnp.float32)
        p[0, :, :, LAYERS : LAYERS + DEPTH, :] = jnp.zeros((3, ROWS, DEPTH, NR), jnp.float32)

    def face(a, c, scale=1.0):
        return (2.0 * scale) * a * c / jnp.maximum(a + c, 0.25)

    def send_row(row, group, slots, send, recv):
        n_others = slots.shape[0] - 1
        slots[n_others] = row

        @pl.loop(0, n_others)
        def _(n):
            pltpu.make_async_remote_copy(
                src_ref=slots.at[n_others],
                dst_ref=slots.at[n],
                send_sem=send,
                recv_sem=recv,
                device_id=group(n),
                device_id_type=MESH,
            ).start()

    def received(slots, send, recv):
        others = slots.at[0 : slots.shape[0] - 1]
        pltpu.make_async_copy(others, others, recv).wait()
        pltpu.make_async_copy(others, others, send).wait()
        return jnp.sum(slots[...], axis=0)

    local[0].wait()
    local[2].wait()
    k_row[0, lay, :] = face(st[0, lay, :], st[1, lay, :])

    def powers_of(i, total):
        k = face(st[i, lay, :], st[i + 1, lay, :])
        d = me[i, lay, :] + 6.0 * (k + k_row[i - 1, lay, :])
        k_row[i, lay, :] = k
        d = d * d
        d = d * d
        return total + d * d

    powers = lax.fori_loop(1, CA - 1, powers_of, jnp.zeros((LAYERS, NR), jnp.float32), unroll=True)
    total = jnp.sum(jnp.sum(powers, axis=0, keepdims=True), axis=1, keepdims=True)
    pl.semaphore_wait(barrier, 2 + size_a + size_b)

    send_row(jnp.broadcast_to(total, (1, 128)), group_a, early_a, red_sem.at[0], red_sem.at[1])
    downward(u_down, st_down)
    upward(u_up, st_up)
    for copy in (u_first, u_last):
        copy.start()
    for copy in (st_first, st_last):
        copy.start()
    downward(me_down)
    upward(me_up)
    pack[...] = jnp.zeros_like(pack)
    me[CA + DEPTH - 1 : CA + DEPTH + 1, lay, :] = jnp.zeros((2, LAYERS, NR), jnp.float32)
    for copy in small:
        copy.wait()
    pack[0:1, 0:4] = nodes[...].astype(jnp.float32)
    pack[1:2, 0:4] = sticks[...].astype(jnp.float32)
    pack[2:4, 0:4] = slips[...]
    pack[4:6, 0:4] = olds[...]
    pack[6:7, 0:4] = weighs[...]

    for slot in range(1, N_BAND):

        @pl.when(b == slot)
        def _():
            pack_copy(slot).start()


    lane = lax.broadcasted_iota(jnp.int32, (LEV, NR), 1)

    def conductances_of(i, scale=1.0):
        a = st[i]
        ku = face(a, pltpu.roll(a, LEV - 1, 0), scale)
        ko = jnp.where(lane == NR - 1, 0.0, face(a, pltpu.roll(a, NR - 1, 1), scale))
        k_up[i] = ku
        k_dn[i] = pltpu.roll(ku, 1, 0)
        k_out[i] = ko
        k_in[i] = pltpu.roll(ko, 1, 1)

    from_bands([u_down, st_down], [u_up, st_up])

    @pl.loop(0, CA)
    def _(i):
        conductances_of(i)

    local[1].wait()
    local[3].wait()

    gains = (1.0, 1.0, 2.0)

    @pl.loop(0, CA)
    def _(i):
        up, dn = jnp.minimum(i + 1, CA - 1), jnp.maximum(i - 1, 0)
        kr_up = k_row[jnp.minimum(i, CA - 2), lay, :]
        kr_dn = k_row[dn, lay, :]
        ku, kd, ko, ki = k_up[i, lay, :], k_dn[i, lay, :], k_out[i, lay, :], k_in[i, lay, :]
        m = me[i, lay, :]
        for c in range(3):
            whole = u[c, i]
            v = whole[0:LAYERS]
            above_v = pltpu.roll(whole, LEV - 1, 0)[0:LAYERS]
            below_v = pltpu.roll(whole, 1, 0)[0:LAYERS]
            acc = ku * (above_v - v) + kd * (below_v - v)
            acc = acc + ko * (pltpu.roll(v, NR - 1, 1) - v) + ki * (pltpu.roll(v, 1, 1) - v)
            acc = acc + kr_up * (u[c, up, lay, :] - v) + kr_dn * (u[c, dn, lay, :] - v)
            p[0, c, i, lay, :] = p[0, c, i, lay, :] - m * v + gains[c] * acc
    for copy in (p_first, p_last, me_first, me_last):
        copy.start()
    send_row(received(early_a, red_sem.at[0], red_sem.at[1]), group_b, early_b, red_sem.at[2], red_sem.at[3])

    @pl.when(low)
    def _():
        packs[0] = pack[...]
        for slot in range(1, N_BAND):
            pack_copy(slot).wait_recv()
        t = packs[0]
        for slot in range(1, N_BAND):
            t = t + pltpu.roll(packs[slot], 4 * slot, 1)
        t = t[:, 0:128]
        node = t[0:1, :].astype(jnp.int32)
        stick = t[1:2, :] > 0.5
        row_of = node // NR
        col_of = lax.rem(node, NR)
        real = lax.broadcasted_iota(jnp.int32, (1, 128), 1) < 4 * N_BAND
        col_hot = jnp.where(
            jnp.logical_and(lax.broadcasted_iota(jnp.int32, (NR, 128), 0) == col_of, real), 1.0, 0.0
        ).astype(jnp.float32)
        row_hot = jnp.where(lax.broadcasted_iota(jnp.int32, (CA, 128), 0) == row_of, 1.0, 0.0).astype(jnp.float32)
        raft = jnp.concatenate([u[c, r, 0:1, :] for c in range(3) for r in range(CA)], axis=0)
        picked = jnp.dot(raft, col_hot, precision=HIGHEST, preferred_element_type=jnp.float32)
        at = [jnp.sum(picked[CA * c : CA * (c + 1)] * row_hot, axis=0, keepdims=True) for c in range(3)]
        trial = [K_STICK * (at[c] - t[2 + c : 3 + c]) for c in range(2)]
        rate = [RATE_GAIN * (at[c] - t[4 + c : 5 + c]) for c in range(2)]
        speed = jnp.sqrt(rate[0] * rate[0] + rate[1] * rate[1] + V_FLOOR * V_FLOOR)
        friction = MU_FAST - (MU_FAST - MU_SLOW) * jnp.exp(-RATE_DECAY * speed)
        capacity = friction * t[6:7]
        magnitude = jnp.sqrt(trial[0] * trial[0] + trial[1] * trial[1])
        largest = jnp.maximum(magnitude, capacity)
        largest = jnp.where(real, largest, 1.0)
        force = [jnp.where(stick, trial[c], capacity * trial[c] / largest) for c in range(2)]
        force = [jnp.where(real, f, 0.0) for f in force + [K_VERT * at[2]]]
        stick_k = jnp.where(jnp.logical_and(stick, real), K_STICK, 0.0)
        vert_k = jnp.where(real, K_VERT, 0.0)
        weights = jnp.concatenate([row_hot * v for v in force + [stick_k, vert_k]], axis=0)
        spread = lax.dot_general(
            weights, col_hot, (((1,), (1,)), ((), ())), precision=HIGHEST, preferred_element_type=jnp.float32
        )
        for n in range(5):
            bear[n, 0:CA] = spread[CA * n : CA * (n + 1)]
        tile = jnp.concatenate(force + [jnp.zeros((5, 128), jnp.float32)], axis=0)
        force_in[...] = tile
        for slot in range(1, N_BAND):
            forces[slot] = pltpu.roll(tile, 128 - 4 * slot, 1)
        for slot in range(1, N_BAND):
            force_copy(slot).start()

    @pl.when(jnp.logical_not(low))
    def _():
        bear[:, 0:CA, :] = jnp.zeros((5, CA, NR), jnp.float32)

    bd_first.start()
    bd_last.start()


    for copy in (st_first, st_last):
        copy.wait_recv()
    downward(st_rim_down)
    upward(st_rim_up)

    for copy in (u_first, u_last):
        copy.wait_recv()
    for copy in (p_first, p_last):
        copy.wait_send()
    for copy in (p_first, p_last):
        copy.wait_recv()
    for here, there in ((CA - 1, CA), (0, ROWS - 1)):
        k = face(st[here, lay, :], st[there, lay, :])
        for c in range(3):
            flux = gains[c] * k * (u[c, there, lay, :] - u[c, here, lay, :])
            p[0, c, here, lay, :] = p[0, c, here, lay, :] + flux
            p[0, c, there, lay, :] = p[0, c, there, lay, :] - flux
    downward(*p_down)
    upward(*p_up)
    for copy in (me_first, me_last):
        copy.wait_recv()
    downward(me_rim_down)
    upward(me_rim_up)

    mean = received(early_b, red_sem.at[2], red_sem.at[3]) * (1.0 / (N_SECTOR * N_BAND * (CA - 2) * LAYERS * NR))
    e128 = jnp.sqrt(jnp.sqrt(jnp.sqrt(mean)))
    scale128 = 2.0 / e128
    scale = jnp.concatenate([scale128, scale128], axis=1)
    from_bands([st_rim_down], [st_rim_up])
    lev = lax.broadcasted_iota(jnp.int32, (LEV, NR), 0)

    @pl.loop(0, ROWS)
    def _(i):
        conductances_of(i, scale)
        k_row[i] = face(st[i], st[lax.rem(i + 1, ROWS)], scale)

    for copy in (bd_first, bd_last):
        copy.wait_recv()

    @pl.when(low)
    def _():
        for c in range(3):
            for i in range(ROWS):
                p[0, c, i, 0:1, :] = p[0, c, i, 0:1, :] - bear[c, i : i + 1, :]

    from_bands([me_down, me_rim_down], [me_up, me_rim_up])

    @pl.loop(0, ROWS)
    def _(i):
        near = k_up[i] + k_dn[i] + k_out[i] + k_in[i] + k_row[i] + k_row[lax.rem(i + ROWS - 1, ROWS)]
        base = scale * me[i] - 2.0
        for h in range(2):
            extra = scale * bear[3 + h, pl.ds(i, 1), :]
            diag[h, i] = base + (h + 1.0) * near + jnp.where(lev == 0, extra, 0.0)

    from_bands(p_down, p_up)

    sums = {}

    def one_row(j, i, tall=slice(0, LEV)):
        up, dn = lax.rem(i + 1, ROWS), lax.rem(i + ROWS - 1, ROWS)
        kr_up, kr_dn, ku, kd, ko, ki = [
            k[n, tall, :] for k, n in ((k_row, i), (k_row, dn), (k_up, i), (k_dn, i), (k_out, i), (k_in, i))
        ]
        out = []
        for c in range(3):
            whole = p[j, c, i]
            v = whole[tall]
            near = ku * pltpu.roll(whole, LEV - 1, 0)[tall] + kd * pltpu.roll(whole, 1, 0)[tall]
            near = near + ko * pltpu.roll(v, NR - 1, 1) + ki * pltpu.roll(v, 1, 1)
            near = near + kr_up * p[j, c, up, tall, :] + kr_dn * p[j, c, dn, tall, :]
            if c == 2:
                near = near + near
            w = diag[c // 2, i, tall, :] * v - near
            w = 0.5 * w if j == 0 else w - p[j - 1, c, i, tall, :]
            p[j + 1, c, i, tall, :] = w
            out.append(w)
        return out

    for j in range(ITERS):
        pairs = [q for q in PAIRS if q[1] == j + 1 or (j == 0 and q == (0, 0))]

        def own_row(i, acc):
            new = one_row(j, i, lay if j == ITERS - 1 else slice(0, LEV))
            acc = list(acc)
            for c in range(3):
                w = new[c][0:LAYERS]
                for n, (lo, hi) in enumerate(pairs):
                    a = w if lo == j + 1 else p[lo, c, i, lay, :]
                    d = w if hi == j + 1 else p[hi, c, i, lay, :]
                    acc[n] = acc[n] + a * d
            return tuple(acc)

        totals = lax.fori_loop(0, CA, own_row, tuple(jnp.zeros((LAYERS, NR), jnp.float32) for _ in pairs), unroll=2)
        sums.update(zip(pairs, totals))
        wide = ITERS - 1 - j
        if wide:

            @pl.loop(0, 2 * wide, unroll=2)
            def _(i):
                one_row(j, jnp.where(i < wide, CA + i, ROWS - 1 - (i - wide)))

    rows = []
    for q in PAIRS:
        t = jnp.sum(sums[q], axis=0, keepdims=True)
        rows.append(t[:, 0:128] + t[:, 128:256])
    rows = jnp.concatenate(rows + [jnp.zeros((16 - len(PAIRS), 128), jnp.float32)], axis=0)
    eye = lax.broadcasted_iota(jnp.int32, (16, 128), 0) == lax.broadcasted_iota(jnp.int32, (16, 128), 1)
    row = jnp.sum(jnp.where(eye, jnp.sum(rows, axis=1, keepdims=True), 0.0), axis=0, keepdims=True)
    send_row(row, group_a, late_a, red_sem.at[4], red_sem.at[5])
    row = received(late_a, red_sem.at[4], red_sem.at[5])
    send_row(row, group_b, late_b, red_sem.at[6], red_sem.at[7])
    row = received(late_b, red_sem.at[6], red_sem.at[7])
    g = jnp.broadcast_to(jnp.sum(jnp.where(eye, row, 0.0), axis=1, keepdims=True), (16, 128))
    where = {q: n for n, q in enumerate(PAIRS)}
    grams = {q: g[where[q] : where[q] + 1, :] for q in PAIRS}
    xs, rs = coefficients(lambda i, j: grams[(i, j)], e128)
    for n, v in enumerate(xs + rs):
        coef_ref[n : n + 1, :] = v

    @pl.when(jnp.logical_not(low))
    def _():
        force_copy(1).wait_recv()

    force_ref[...] = force_in[...]

    for slot in range(1, N_BAND):

        @pl.when(b == slot)
        def _():
            pack_copy(slot).wait_send()

    @pl.when(low)
    def _():
        for slot in range(1, N_BAND):
            force_copy(slot).wait_send()

    for copy in (st_first, st_last, u_first, u_last, me_first, me_last, bd_first, bd_last):
        copy.wait_send()

    @pl.when(jnp.logical_not(low))
    def _():
        for copy in [u_down, st_down, me_down, st_rim_down, me_rim_down] + p_down:
            copy.wait_send()

    @pl.when(jnp.logical_not(high))
    def _():
        for copy in [u_up, st_up, me_up, st_rim_up, me_rim_up] + p_up:
            copy.wait_send()


def combine(p, coef, force, inc_hbm, res_hbm, force_hbm, inc, res, out, sems):
    out[...] = force[0:3, 0:4]
    copies = [pltpu.make_async_copy(out, force_hbm, sems.at[0])]
    copies[0].start()
    rows = [jnp.concatenate([coef[n : n + 1, :]] * 2, axis=1) for n in range(2 * ITERS + 1)]
    xs, rs = rows[:ITERS], rows[ITERS:]
    step = CA // 4

    @pl.loop(0, 4)
    def _(chunk):
        for k in range(step):
            i = chunk * step + k
            for c in range(3):
                vs = [p[j, c, i, 0:LAYERS, :] for j in range(ITERS + 1)]
                a, r = xs[0] * vs[0], rs[0] * vs[0]
                for j in range(1, ITERS):
                    a = a + xs[j] * vs[j]
                for j in range(1, ITERS + 1):
                    r = r + rs[j] * vs[j]
                inc[c, i] = a
                res[c, i] = r
        span = pl.ds(chunk * step, step)
        for n, (src, dst) in enumerate(((inc, inc_hbm), (res, res_hbm))):
            pltpu.make_async_copy(src.at[:, span], dst.at[:, span], sems.at[1 + n]).start()

    copies.append(pltpu.make_async_copy(inc, inc_hbm, sems.at[1]))
    copies.append(pltpu.make_async_copy(res, res_hbm, sems.at[2]))
    for copy in copies:
        copy.wait()


def per_device(
    given_load,
    displacement,
    mass_coef,
    stiffness,
    bearing_node,
    stick_state,
    slip_prev,
    bearing_old,
    bearing_weight,
):
    f32, i32 = jnp.float32, jnp.int32
    vmem, dma = pltpu.VMEM, pltpu.SemaphoreType.DMA
    field = jax.ShapeDtypeStruct((3, CA, LAYERS, NR), f32)
    in_vmem = pl.BlockSpec(memory_space=vmem)
    in_hbm = pl.BlockSpec(memory_space=pltpu.HBM)
    basis, coef, force = pl.pallas_call(
        kernel,
        out_shape=(
            jax.ShapeDtypeStruct((ITERS + 1, 3, ROWS, LEV, NR), f32),
            jax.ShapeDtypeStruct((16, 128), f32),
            jax.ShapeDtypeStruct((8, 128), f32),
        ),
        in_specs=[in_hbm] * 9,
        out_specs=(in_vmem, in_vmem, in_vmem),
        scratch_shapes=[
            vmem((ROWS, LEV, NR), f32),
            vmem((ROWS, LEV, NR), f32),
            vmem((3, ROWS, LEV, NR), f32),
            vmem((ROWS, LEV, NR), f32),
            vmem((ROWS, LEV, NR), f32),
            vmem((ROWS, LEV, NR), f32),
            vmem((ROWS, LEV, NR), f32),
            vmem((ROWS, LEV, NR), f32),
            vmem((2, ROWS, LEV, NR), f32),
            vmem((5, ROWS, NR), f32),
            vmem((1, 4), i32),
            vmem((1, 4), i32),
            vmem((2, 4), f32),
            vmem((2, 4), f32),
            vmem((1, 4), f32),
            vmem((8, 128), f32),
            vmem((N_BAND, 8, 128), f32),
            vmem((N_BAND, 8, 128), f32),
            vmem((8, 128), f32),
            vmem((8, 1, 128), f32),
            vmem((32, 1, 128), f32),
            vmem((8, 1, 128), f32),
            vmem((32, 1, 128), f32),
            dma((9,)),
            dma((26,)),
            dma((26,)),
            dma((N_BAND,)),
            dma((N_BAND,)),
            dma((N_BAND,)),
            dma((1,)),
            dma((8,)),
        ],
        compiler_params=pltpu.CompilerParams(
            collective_id=0, has_side_effects=True, vmem_limit_bytes=32 * 1024 * 1024
        ),
        name="newton_step",
    )(
        *[
            pltpu.with_memory_space_constraint(a, pltpu.HBM)
            for a in (
                given_load,
                displacement,
                mass_coef,
                stiffness,
                bearing_node.reshape(1, 4),
                stick_state.reshape(1, 4),
                slip_prev,
                bearing_old,
                bearing_weight.reshape(1, 4),
            )
        ]
    )
    return pl.pallas_call(
        combine,
        out_shape=(field, field, jax.ShapeDtypeStruct((3, 4), f32)),
        in_specs=[in_vmem] * 3,
        out_specs=(in_hbm, in_hbm, in_hbm),
        scratch_shapes=[
            vmem((3, CA, LAYERS, NR), f32),
            vmem((3, CA, LAYERS, NR), f32),
            vmem((3, 4), f32),
            dma((9,)),
        ],
        compiler_params=pltpu.CompilerParams(vmem_limit_bytes=16 * 1024 * 1024),
        name="combine",
    )(basis, coef, force)


def solution(mesh):
    return jax.shard_map(
        per_device,
        mesh=mesh,
        in_specs=(
            P(None, "sector", "band", None),
            P(None, "sector", "band", None),
            P("sector", "band", None),
            P("sector", "band", None),
            P(("sector", "band")),
            P(("sector", "band")),
            P(None, ("sector", "band")),
            P(None, ("sector", "band")),
            P(("sector", "band")),
        ),
        out_specs=(
            P(None, "sector", "band", None),
            P(None, "sector", "band", None),
            P(None, ("sector", "band")),
        ),
        check_vma=False,
    )
```
